256 devices in a mesh: row: 16 (over y_lo, z), col: 16 (over y_hi, x, core).
Axes of the slice: x: 4, y: 4 (y_hi: 2, y_lo: 2; y = y_hi * 2 + y_lo), z: 8, core: 2. Of those that a mesh axis runs over, the one named last changes fastest.
Arguments:
- early_coords: bfloat16 [64, 32768], P(None, ('row', 'col')), may hold values from -13 to 13
- late_coords: bfloat16 [64, 131072], P(None, ('row', 'col')), may hold values from -13 to 13
- late_log_scale: bfloat16 [131072], P(('row', 'col')), may hold values from -2 to 115
- fate_labels: int32 [32768], P(('row', 'col')), may hold values from 0 to 255, as said below
- loadings: float32 [64, 2000], replicated, may hold values from -0.75 to 0.75
Outputs:
- projected: float32 [64, 32768], P(None, ('row', 'col'))
- fate_corr: float32 [2000, 256], replicated
The draws below stay inside these ranges and needn't reach their ends.
Inputs may be any that keep to these rules, and one draw needn't show every extreme that they name: `fate_labels`: every one of the 256 fate classes labels at least one early cell.
All inputs are finite; a program needn't handle non-finite values.
Results may differ from the reference program's by a relative error of at most 0.0003.
Values may be sent and summed in bfloat16 or wider, within the bound.
No kernel may reach another device: no remote copies, remote signals or barrier semaphores. Data moves between devices by JAX's collectives and lax.ppermute only.
A program may use at most 64 MiB of HBM per device.

```python
import math
import jax
import jax.numpy as jnp
from jax import lax

DIM = 64
GENES = 2000
FATES = 256
EARLY_CELLS = 32768
LATE_CELLS = 131072


def draw_world(key):
    keys = jax.random.split(jax.random.fold_in(key, 4051), 7)
    positions = jnp.arange(EARLY_CELLS, dtype=jnp.int32)
    base = positions * FATES // EARLY_CELLS
    starts = positions == (base * EARLY_CELLS + FATES - 1) // FATES
    jitter = jax.random.randint(keys[0], (EARLY_CELLS,), 0, 4)
    jitter = jnp.where(starts, 0, jitter)
    labels = ((base + jitter) % FATES).astype(jnp.int32)
    centers = jax.random.normal(keys[1], (FATES, DIM), jnp.float32)
    drift = jax.random.normal(keys[2], (FATES, DIM), jnp.float32)
    late_class = jax.random.randint(keys[3], (LATE_CELLS,), 0, FATES)
    early_noise = 0.5 * jax.random.normal(keys[4], (DIM, EARLY_CELLS), jnp.float32)
    late_noise = 0.5 * jax.random.normal(keys[5], (DIM, LATE_CELLS), jnp.float32)
    early = jnp.take(centers, labels, axis=0).T + early_noise
    late = jnp.take(centers + drift, late_class, axis=0).T + late_noise
    log_scale = jax.random.uniform(keys[6], (LATE_CELLS,), jnp.float32, -2.0, 2.0)
    early = jnp.clip(early, -12.9, 12.9)
    late = jnp.clip(late, -12.9, 12.9)
    return (early, late, log_scale, labels)


def draw_early_coords(key, part):
    return draw_world(key)[0].astype(jnp.bfloat16)


def draw_late_coords(key, part):
    return draw_world(key)[1].astype(jnp.bfloat16)


def draw_late_log_scale(key, part):
    return draw_world(key)[2].astype(jnp.bfloat16)


def draw_fate_labels(key, part):
    return draw_world(key)[3]


def gaussian(own_key, dims, width, bound, held_as=jnp.bfloat16):
    values = jax.random.normal(own_key, dims, jnp.float32) * width
    return jnp.minimum(jnp.maximum(values, -bound), bound).astype(held_as)


def setup_inputs(seed: int = 0) -> dict:
    streams_of = jax.random.split(jax.random.key(seed), 6)
    return {
        "early_coords": draw_early_coords(jax.random.fold_in(streams_of[5], 71), 0),
        "late_coords": draw_late_coords(jax.random.fold_in(streams_of[5], 71), 0),
        "late_log_scale": draw_late_log_scale(jax.random.fold_in(streams_of[5], 71), 0),
        "fate_labels": draw_fate_labels(jax.random.fold_in(streams_of[5], 71), 0),
        "loadings": gaussian(streams_of[4], (DIM, GENES), DIM ** -0.5, 0.75, jnp.float32),
    }


kernel_ratio = 8.0
epsilon = 1e-06

def reference(early_coords, late_coords, late_log_scale, fate_labels, loadings):
    precise = lax.Precision.HIGHEST
    sharpness = kernel_ratio / DIM
    late_wide = late_coords.astype(jnp.float32)
    late_norms = lax.optimization_barrier(jnp.sum(late_wide * late_wide, 0))
    log_weights = late_log_scale.astype(jnp.float32)
    early_wide = early_coords.astype(jnp.float32)
    stride = math.gcd(EARLY_CELLS, 512)
    blocks = EARLY_CELLS // stride
    grouped = jnp.transpose(early_wide.reshape(DIM, blocks, stride), (1, 0, 2))

    def project(row_slab):
        crossed = jnp.dot(row_slab.T, late_wide, precision=precise)
        slab_norms = lax.optimization_barrier(jnp.sum(row_slab * row_slab, 0))
        distance = slab_norms[:, None] + late_norms[None, :] - 2.0 * crossed
        scores = log_weights[None, :] - distance * sharpness
        row_top = lax.optimization_barrier(jnp.max(scores, 1))
        kernel = jnp.exp(scores - row_top[:, None])
        row_sums = lax.optimization_barrier(jnp.sum(kernel, 1))
        numerators = jnp.dot(late_wide, kernel.T, precision=precise)
        return numerators / row_sums[None, :]
    projected = jnp.transpose(lax.map(project, grouped), (1, 0, 2)).reshape(DIM, EARLY_CELLS)
    displacement = projected - early_wide
    disp_groups = jnp.transpose(displacement.reshape(DIM, blocks, stride), (1, 0, 2))
    label_groups = fate_labels.reshape(blocks, stride)
    classes = jnp.arange(FATES, dtype=jnp.int32)

    def gather_moments(carried, pieces):
        disp_slab, label_slab = pieces
        gene_shift = jnp.dot(loadings.T, disp_slab, precision=precise)
        indicator = (label_slab[None, :] == classes[:, None]).astype(jnp.float32)
        cross_sum = carried[0] + jnp.dot(gene_shift, indicator.T, precision=precise)
        gene_total = carried[1] + lax.optimization_barrier(jnp.sum(gene_shift, 1))
        gene_square = carried[2] + lax.optimization_barrier(jnp.sum(gene_shift * gene_shift, 1))
        fate_count = carried[3] + lax.optimization_barrier(jnp.sum(indicator, 1))
        return ((cross_sum, gene_total, gene_square, fate_count), None)
    start_state = (jnp.zeros((GENES, FATES), jnp.float32), jnp.zeros((GENES,), jnp.float32), jnp.zeros((GENES,), jnp.float32), jnp.zeros((FATES,), jnp.float32))
    sums, unused = lax.scan(gather_moments, start_state, (disp_groups, label_groups))
    cross_sum, gene_total, gene_square, fate_count = sums
    cell_count = float(EARLY_CELLS)
    mean_shift = gene_total / cell_count
    variance = gene_square / cell_count - mean_shift * mean_shift + epsilon
    fate_share = fate_count / cell_count
    spread = fate_share * (1.0 - fate_share)
    covariance = cross_sum / cell_count - mean_shift[:, None] * fate_share[None, :]
    fate_corr = covariance / jnp.sqrt(variance[:, None] * spread[None, :])
    return (projected, fate_corr)
```

```python
import functools
import math

import jax
import jax.numpy as jnp
from jax import lax
from jax.experimental import pallas as pl
from jax.experimental.pallas import tpu as pltpu
from jax.sharding import Mesh
from jax.sharding import PartitionSpec as P

f32 = jnp.float32
bf16 = jnp.bfloat16

DIM = 64
FATES = 256
EPSILON = 1e-06
SHARP = 8.0 / DIM
LOG2E = math.log2(math.e)
LOWEST = -1e30

AXES = ("yl", "z", "yh", "x", "core")
SIZES = (2, 8, 2, 4, 2)
EARLY_GROUP = ("yl", "yh", "x")
LATE_GROUP = ("z", "core")


def split3(v):
    high = v.astype(bf16).astype(f32)
    rest = v - high
    mid = rest.astype(bf16).astype(f32)
    return high, mid, rest - mid


def put_rows(base, row, first, value):
    for k, piece in enumerate(split3(value)):
        base = jnp.where(row == first + k, piece, base)
    return base


def attention_kernel(x_ref, y_ref, out_ref, xa, ya, yw, sbuf, mbuf, acc, *, tile, sub):
    n_early, _, early_width = x_ref.shape
    n_late, _, late_width = y_ref.shape
    pairs = n_early // 2
    tiles = n_late * late_width // tile
    wide = 2 * early_width

    def prepare_early(b, carry):
        x = jnp.concatenate([x_ref[2 * b], x_ref[2 * b + 1]], 1).astype(f32)
        norms = jnp.sum(x * x, 0, keepdims=True)
        high, mid, low = split3(x * (2.0 * SHARP * LOG2E))
        row = lax.broadcasted_iota(jnp.int32, (DIM, wide), 0)
        extra = jnp.where(row < 3, 1.0, jnp.zeros((DIM, wide), f32))
        extra = put_rows(extra, row, 3, norms * (-SHARP * LOG2E))
        xa[b] = jnp.concatenate([high, extra, mid, low], 0).astype(bf16)
        return carry

    lax.fori_loop(0, pairs, prepare_early, 0)

    def prepare_late(b, carry):
        yb = y_ref[b, :DIM, :]
        y = yb.astype(f32)
        logs = y_ref[b, DIM : DIM + 8, :].astype(f32)[:1]
        bias = (logs - jnp.sum(y * y, 0, keepdims=True) * SHARP) * LOG2E
        row = lax.broadcasted_iota(jnp.int32, (DIM, late_width), 0)
        extra = jnp.where((row >= 3) & (row < 6), 1.0, jnp.zeros((DIM, late_width), f32))
        extra = put_rows(extra, row, 0, bias)
        t = jnp.concatenate([y, extra], 0).T
        lane = lax.broadcasted_iota(jnp.int32, (late_width, 128), 1)
        twice = jnp.where(lane < DIM, t, pltpu.roll(t, DIM, 1))
        first = pl.multiple_of(b * late_width, late_width)
        ya[pl.ds(first, late_width), :] = jnp.concatenate([t, twice], 1).astype(bf16)
        ones = jnp.where(lax.broadcasted_iota(jnp.int32, (16, late_width), 0) == 0, 1.0, 0.0)
        yw[:, pl.ds(first, late_width)] = jnp.concatenate([yb, ones.astype(bf16)], 0)
        return carry

    lax.fori_loop(0, n_late, prepare_late, 0)
    acc[...] = jnp.zeros_like(acc)
    parts = tile // sub

    def score_part(pair, first, j, slot, top):
        s = jnp.dot(ya[pl.ds(first + j * sub, sub), :], xa[pair], preferred_element_type=f32)
        sbuf[slot, j * sub : (j + 1) * sub, :] = s
        here = jnp.max(s.reshape(sub // 8, 8, wide), 0)
        return here if top is None else jnp.maximum(top, here)

    steps = pairs * tiles
    top = None
    for j in range(parts):
        top = score_part(0, 0, j, 0, top)
    mbuf[0] = top

    def step(n, slot, before):
        pair = n // tiles
        first = pl.multiple_of((n % tiles) * tile, tile)
        following = jnp.minimum(n + 1, steps - 1)
        next_first = pl.multiple_of((following % tiles) * tile, tile)
        before = jnp.where(n % tiles == 0, LOWEST, before)
        now = jnp.maximum(before, jnp.max(mbuf[slot], 0, keepdims=True))
        shrink = jnp.exp2(before - now)
        top = None
        sums = None
        for j in range(parts):
            top = score_part(following // tiles, next_first, j, 1 - slot, top)
            weights = jnp.exp2(sbuf[slot, j * sub : (j + 1) * sub, :] - now).astype(bf16)
            more = jnp.dot(yw[:, pl.ds(first + j * sub, sub)], weights, preferred_element_type=f32)
            sums = more if sums is None else sums + more
        mbuf[1 - slot] = top
        total = acc[...] * shrink + sums
        acc[...] = total
        row = lax.broadcasted_iota(jnp.int32, (72, wide), 0)
        packed = jnp.where(row == DIM + 1, now, total[:72])
        out_ref[2 * pair] = packed[:, :early_width]
        out_ref[2 * pair + 1] = packed[:, early_width:]
        return now

    def two_steps(i, before):
        return step(2 * i + 1, 1, step(2 * i, 0, before))

    lax.fori_loop(0, steps // 2, two_steps, jnp.full((1, wide), LOWEST, f32))


def attention(early_all, late_all, tile=2048, sub=512):
    n_early, _, early_width = early_all.shape
    n_late, _, late_width = late_all.shape
    late_total = n_late * late_width
    wide = 2 * early_width
    return pl.pallas_call(
        functools.partial(attention_kernel, tile=tile, sub=sub),
        out_shape=jax.ShapeDtypeStruct((n_early, 72, early_width), f32),
        in_specs=[pl.BlockSpec(memory_space=pltpu.VMEM)] * 2,
        out_specs=pl.BlockSpec(memory_space=pltpu.VMEM),
        scratch_shapes=[
            pltpu.VMEM((n_early // 2, 256, wide), bf16),
            pltpu.VMEM((late_total, 256), bf16),
            pltpu.VMEM((80, late_total), bf16),
            pltpu.VMEM((2, tile, wide), f32),
            pltpu.VMEM((2, 8, wide), f32),
            pltpu.VMEM((80, wide), f32),
        ],
        compiler_params=pltpu.CompilerParams(vmem_limit_bytes=48 * 2**20),
        name="attention",
    )(early_all, late_all)


def moments_kernel(got_ref, x_ref, label_ref, projected_ref, sums_ref):
    peers, _, cells = got_ref.shape
    top = got_ref[0, DIM : DIM + 8, :][1:2]
    for p in range(1, peers):
        top = jnp.maximum(top, got_ref[p, DIM : DIM + 8, :][1:2])
    total = jnp.zeros((72, cells), f32)
    for p in range(peers):
        block = got_ref[p]
        total = total + block * jnp.exp2(block[DIM + 1 : DIM + 2] - top)
    projected = total[:DIM] / total[DIM : DIM + 1]
    projected_ref[...] = projected
    moved = projected - x_ref[...].astype(f32)
    classes = lax.broadcasted_iota(jnp.int32, (FATES, cells), 0)
    indicator = jnp.where(classes == label_ref[...], 1.0, 0.0)
    across = (((1,), (1,)), ((), ()))
    by_class = lax.dot_general(
        moved, indicator, across, precision=lax.Precision.HIGHEST, preferred_element_type=f32
    )
    padded = jnp.concatenate([moved, jnp.zeros((128 - DIM, cells), f32)], 0)
    second = lax.dot_general(
        moved, padded, across, precision=lax.Precision.HIGHEST, preferred_element_type=f32
    )
    count = jnp.sum(indicator, 1, keepdims=True)
    lane = lax.broadcasted_iota(jnp.int32, (DIM, 128), 1)
    for q in range(FATES // DIM):
        second = jnp.where(lane == DIM + q, count[DIM * q : DIM * (q + 1)], second)
    sums_ref[:8] = by_class.reshape(8, 8, FATES)
    sums_ref[8:] = jnp.concatenate([second, jnp.zeros((DIM, 128), f32)], 1).reshape(8, 8, FATES)


def moments(got, early, labels):
    return pl.pallas_call(
        moments_kernel,
        out_shape=(
            jax.ShapeDtypeStruct(early.shape, f32),
            jax.ShapeDtypeStruct((16, 8, FATES), f32),
        ),
        in_specs=[pl.BlockSpec(memory_space=pltpu.VMEM)] * 3,
        out_specs=(pl.BlockSpec(memory_space=pltpu.VMEM),) * 2,
        name="moments",
    )(got, early, labels)


def correlate_kernel(sums_ref, split_ref, plain_ref, out_ref, right, *, cells):
    @pl.when(pl.program_id(0) == 0)
    def _():
        by_class = sums_ref[:8].reshape(DIM, FATES) / cells
        second = sums_ref[8:].reshape(DIM, FATES)[:, :128]
        flipped = second.T
        share = jnp.concatenate(
            [flipped[DIM + q : DIM + q + 1] for q in range(FATES // DIM)], 1
        ) / cells
        mean = jnp.sum(by_class, 1, keepdims=True)
        mean_row = jnp.broadcast_to(mean, (DIM, 128)).T[:1]
        mean_row = jnp.concatenate([mean_row, jnp.zeros((1, 128 - DIM), f32)], 1)
        lane = lax.broadcasted_iota(jnp.int32, (DIM, 128), 1)
        square = jnp.where(lane < DIM, second, 0.0) / cells - mean * mean_row
        cross = (by_class - mean * share) / jnp.sqrt(share * (1.0 - share))
        both = jnp.concatenate([cross, square], 1)
        high = both.astype(bf16)
        low = (both - high.astype(f32)).astype(bf16)
        right[...] = jnp.concatenate([high, high, low, low], 0)

    product = jnp.dot(split_ref[...], right[...], preferred_element_type=f32)
    variance = jnp.sum(product[:, FATES:] * plain_ref[...], 1, keepdims=True) + EPSILON
    out_ref[...] = product[:, :FATES] * (1.0 / jnp.sqrt(variance))


def correlate(sums, split, plain, cells, block=400):
    genes = split.shape[0]
    return pl.pallas_call(
        functools.partial(correlate_kernel, cells=cells),
        grid=(genes // block,),
        out_shape=jax.ShapeDtypeStruct((genes, FATES), f32),
        in_specs=[
            pl.BlockSpec((16, 8, FATES), lambda i: (0, 0, 0)),
            pl.BlockSpec((block, 256), lambda i: (i, 0)),
            pl.BlockSpec((block, 128), lambda i: (i, 0)),
        ],
        out_specs=pl.BlockSpec((block, FATES), lambda i: (i, 0)),
        scratch_shapes=[pltpu.VMEM((256, FATES + 128), bf16)],
        name="correlate",
    )(sums, split, plain)


def exchange(blocks, axes):
    return lax.all_to_all(blocks, axes, 0, 0, tiled=False)


def spread(block, axes):
    return exchange(jnp.broadcast_to(block[None], (16,) + block.shape), axes)


def per_device(early, late, late_logs, labels, loadings):
    cells = float(early.shape[1] * math.prod(SIZES))
    turned = loadings.T
    high = lax.reduce_precision(turned, 8, 7)
    low = turned - high
    split = jnp.concatenate([high, low, high, low], 1).astype(bf16)
    plain = jnp.pad(turned, ((0, 0), (0, 128 - DIM)))

    late_full = jnp.concatenate([late, late_logs[None], jnp.zeros((7,) + late_logs.shape, bf16)], 0)
    early_all = spread(early, EARLY_GROUP)
    late_all = spread(late_full, LATE_GROUP)
    partial = attention(early_all, late_all)
    got = exchange(partial, EARLY_GROUP)
    projected, sums = moments(got, early, labels[None])
    sums = jnp.sum(exchange(sums, EARLY_GROUP), 0)
    sums = jnp.sum(spread(sums, LATE_GROUP), 0)
    sums = spread(sums, EARLY_GROUP)
    return projected, correlate(sums, split, plain, cells)


def solution(mesh):
    named = Mesh(mesh.devices.reshape(SIZES), AXES)
    in_specs = (P(None, AXES), P(None, AXES), P(AXES), P(AXES), P())
    out_specs = (P(None, AXES), P())
    return jax.shard_map(
        per_device, mesh=named, in_specs=in_specs, out_specs=out_specs, check_vma=False
    )
```

```python
import functools
import math

import jax
import jax.numpy as jnp
from jax import lax
from jax.experimental import pallas as pl
from jax.experimental.pallas import tpu as pltpu
from jax.sharding import Mesh
from jax.sharding import PartitionSpec as P


f32 = jnp.float32
bf16 = jnp.bfloat16

DIM = 64
FATES = 256
EPSILON = 1e-06
SHARP = 8.0 / DIM
LOG2E = math.log2(math.e)
LOWEST = -1e30

AXES = ("yl", "z", "yh", "x", "core")
SIZES = (2, 8, 2, 4, 2)
EARLY_GROUP = ("yl", "yh", "x")
LATE_GROUP = ("z", "core")


def split3(v):
    high = v.astype(bf16).astype(f32)
    rest = v - high
    mid = rest.astype(bf16).astype(f32)
    return high, mid, rest - mid


def put_rows(base, row, first, value):
    for k, piece in enumerate(split3(value)):
        base = jnp.where(row == first + k, piece, base)
    return base


def attention_kernel(x_ref, own_ref, other_ref, out_ref, xa, ya, yw, sbuf, mbuf, acc, *, tile, sub):
    n_early, _, early_width = x_ref.shape
    n_half, _, late_width = own_ref.shape
    n_late = 2 * n_half
    pairs = n_early // 2
    tiles = n_late * late_width // tile
    wide = 2 * early_width

    def prepare_early(b, carry):
        x = jnp.concatenate([x_ref[2 * b], x_ref[2 * b + 1]], 1).astype(f32)
        norms = jnp.sum(x * x, 0, keepdims=True)
        high, mid, low = split3(x * (2.0 * SHARP * LOG2E))
        row = lax.broadcasted_iota(jnp.int32, (DIM, wide), 0)
        extra = jnp.where(row < 3, 1.0, jnp.zeros((DIM, wide), f32))
        extra = put_rows(extra, row, 3, norms * (-SHARP * LOG2E))
        xa[b] = jnp.concatenate([high, extra, mid, low], 0).astype(bf16)
        return carry

    lax.fori_loop(0, pairs, prepare_early, 0)

    def prepare_late(y_ref, b, slot):
        yb = y_ref[b, :DIM, :]
        y = yb.astype(f32)
        logs = y_ref[b, DIM : DIM + 8, :].astype(f32)[:1]
        bias = (logs - jnp.sum(y * y, 0, keepdims=True) * SHARP) * LOG2E
        row = lax.broadcasted_iota(jnp.int32, (DIM, late_width), 0)
        extra = jnp.where((row >= 3) & (row < 6), 1.0, jnp.zeros((DIM, late_width), f32))
        extra = put_rows(extra, row, 0, bias)
        t = jnp.concatenate([y, extra], 0).T
        lane = lax.broadcasted_iota(jnp.int32, (late_width, 128), 1)
        twice = jnp.where(lane < DIM, t, pltpu.roll(t, DIM, 1))
        first = pl.multiple_of(slot * late_width, late_width)
        ya[pl.ds(first, late_width), :] = jnp.concatenate([t, twice], 1).astype(bf16)
        ones = jnp.where(lax.broadcasted_iota(jnp.int32, (16, late_width), 0) == 0, 1.0, 0.0)
        yw[:, pl.ds(first, late_width)] = jnp.concatenate([yb, ones.astype(bf16)], 0)

    def prepare_both(b, carry):
        prepare_late(own_ref, b, b)
        prepare_late(other_ref, b, n_half + b)
        return carry

    lax.fori_loop(0, n_half, prepare_both, 0)
    acc[...] = jnp.zeros_like(acc)
    parts = tile // sub

    def score_part(pair, first, j, slot, top):
        s = jnp.dot(ya[pl.ds(first + j * sub, sub), :], xa[pair], preferred_element_type=f32)
        sbuf[slot, j * sub : (j + 1) * sub, :] = s
        here = jnp.max(s.reshape(sub // 8, 8, wide), 0)
        return here if top is None else jnp.maximum(top, here)

    steps = pairs * tiles
    top = None
    for j in range(parts):
        top = score_part(0, 0, j, 0, top)
    mbuf[0] = top

    def step(n, slot, before):
        pair = n // tiles
        first = pl.multiple_of((n % tiles) * tile, tile)
        following = jnp.minimum(n + 1, steps - 1)
        next_first = pl.multiple_of((following % tiles) * tile, tile)
        before = jnp.where(n % tiles == 0, LOWEST, before)
        now = jnp.maximum(before, jnp.max(mbuf[slot], 0, keepdims=True))
        shrink = jnp.exp2(before - now)
        top = None
        sums = None
        for j in range(parts):
            top = score_part(following // tiles, next_first, j, 1 - slot, top)
            weights = jnp.exp2(sbuf[slot, j * sub : (j + 1) * sub, :] - now).astype(bf16)
            more = jnp.dot(yw[:, pl.ds(first + j * sub, sub)], weights, preferred_element_type=f32)
            sums = more if sums is None else sums + more
        mbuf[1 - slot] = top
        total = acc[...] * shrink + sums
        acc[...] = total
        row = lax.broadcasted_iota(jnp.int32, (72, wide), 0)
        packed = jnp.where(row == DIM + 1, now, total[:72])
        out_ref[2 * pair] = packed[:, :early_width]
        out_ref[2 * pair + 1] = packed[:, early_width:]
        return now

    def two_steps(i, before):
        return step(2 * i + 1, 1, step(2 * i, 0, before))

    lax.fori_loop(0, steps // 2, two_steps, jnp.full((1, wide), LOWEST, f32))


def attention(early_all, late_own, late_other, tile=2048, sub=512):
    n_early, _, early_width = early_all.shape
    n_half, _, late_width = late_own.shape
    late_total = 2 * n_half * late_width
    wide = 2 * early_width
    return pl.pallas_call(
        functools.partial(attention_kernel, tile=tile, sub=sub),
        out_shape=jax.ShapeDtypeStruct((n_early, 72, early_width), f32),
        in_specs=[pl.BlockSpec(memory_space=pltpu.VMEM)] * 3,
        out_specs=pl.BlockSpec(memory_space=pltpu.VMEM),
        scratch_shapes=[
            pltpu.VMEM((n_early // 2, 256, wide), bf16),
            pltpu.VMEM((late_total, 256), bf16),
            pltpu.VMEM((80, late_total), bf16),
            pltpu.VMEM((2, tile, wide), f32),
            pltpu.VMEM((2, 8, wide), f32),
            pltpu.VMEM((80, wide), f32),
        ],
        compiler_params=pltpu.CompilerParams(vmem_limit_bytes=48 * 2**20),
        name="attention",
    )(early_all, late_own, late_other)


def moments_kernel(got_ref, x_ref, label_ref, projected_ref, sums_ref):
    peers, _, cells = got_ref.shape
    top = got_ref[0, DIM : DIM + 8, :][1:2]
    for p in range(1, peers):
        top = jnp.maximum(top, got_ref[p, DIM : DIM + 8, :][1:2])
    total = jnp.zeros((72, cells), f32)
    for p in range(peers):
        block = got_ref[p]
        total = total + block * jnp.exp2(block[DIM + 1 : DIM + 2] - top)
    projected = total[:DIM] / total[DIM : DIM + 1]
    projected_ref[...] = projected
    moved = projected - x_ref[...].astype(f32)
    classes = lax.broadcasted_iota(jnp.int32, (FATES, cells), 0)
    indicator = jnp.where(classes == label_ref[...], 1.0, 0.0)
    across = (((1,), (1,)), ((), ()))
    by_class = lax.dot_general(
        moved, indicator, across, precision=lax.Precision.HIGHEST, preferred_element_type=f32
    )
    padded = jnp.concatenate([moved, jnp.zeros((128 - DIM, cells), f32)], 0)
    second = lax.dot_general(
        moved, padded, across, precision=lax.Precision.HIGHEST, preferred_element_type=f32
    )
    count = jnp.sum(indicator, 1, keepdims=True)
    lane = lax.broadcasted_iota(jnp.int32, (DIM, 128), 1)
    for q in range(FATES // DIM):
        second = jnp.where(lane == DIM + q, count[DIM * q : DIM * (q + 1)], second)
    sums_ref[:8] = by_class.reshape(8, 8, FATES)
    sums_ref[8:] = jnp.concatenate([second, jnp.zeros((DIM, 128), f32)], 1).reshape(8, 8, FATES)


def moments(got, early, labels):
    return pl.pallas_call(
        moments_kernel,
        out_shape=(
            jax.ShapeDtypeStruct(early.shape, f32),
            jax.ShapeDtypeStruct((16, 8, FATES), f32),
        ),
        in_specs=[pl.BlockSpec(memory_space=pltpu.VMEM)] * 3,
        out_specs=(pl.BlockSpec(memory_space=pltpu.VMEM),) * 2,
        compiler_params=pltpu.CompilerParams(vmem_limit_bytes=16 * 2**20),
        name="moments",
    )(got, early, labels)


def correlate_kernel(sums_ref, split_ref, out_ref, right, stage, sems, *, cells, block):
    genes = split_ref.shape[0]
    by_class = sums_ref[:8].reshape(DIM, FATES) / cells
    second = sums_ref[8:].reshape(DIM, FATES)[:, :128]
    flipped = second.T
    share = jnp.concatenate([flipped[DIM + q : DIM + q + 1] for q in range(FATES // DIM)], 1) / cells
    mean = jnp.sum(by_class, 1, keepdims=True)
    mean_row = jnp.broadcast_to(mean, (DIM, 128)).T[:1, :DIM]
    square = second[:, :DIM] / cells - mean * mean_row
    cross = (by_class - mean * share) / jnp.sqrt(share * (1.0 - share))
    both = jnp.concatenate([cross, square, square], 1)
    high = both.astype(bf16)
    low = (both - high.astype(f32)).astype(bf16)
    right[...] = jnp.concatenate([high, high, low, low], 0)

    def copy(k):
        rows = pl.ds(k * block, block)
        return pltpu.make_async_copy(stage.at[rows], out_ref.at[rows], sems.at[k])

    for k in range(genes // block):
        rows = split_ref[k * block : (k + 1) * block]
        product = jnp.dot(rows, right[...], preferred_element_type=f32)
        halves = rows[:, :128].astype(f32)
        variance = jnp.sum(product[:, FATES:] * halves, 1, keepdims=True) + EPSILON
        stage[k * block : (k + 1) * block] = product[:, :FATES] * (1.0 / jnp.sqrt(variance))
        copy(k).start()
    for k in range(genes // block):
        copy(k).wait()


def correlate(sums, split, cells, block=400):
    genes = split.shape[0]
    return pl.pallas_call(
        functools.partial(correlate_kernel, cells=cells, block=block),
        out_shape=jax.ShapeDtypeStruct((genes, FATES), f32),
        in_specs=[pl.BlockSpec(memory_space=pltpu.VMEM)] * 2,
        out_specs=pl.BlockSpec(memory_space=pl.ANY),
        scratch_shapes=[
            pltpu.VMEM((256, FATES + 128), bf16),
            pltpu.VMEM((genes, FATES), f32),
            pltpu.SemaphoreType.DMA((genes // block,)),
        ],
        compiler_params=pltpu.CompilerParams(vmem_limit_bytes=16 * 2**20),
        name="correlate",
    )(sums, split)


def exchange(blocks, axes):
    return lax.all_to_all(blocks, axes, 0, 0, tiled=False)


def spread(block, axes):
    return exchange(jnp.broadcast_to(block[None], (16,) + block.shape), axes)


def program(early, late, late_logs, labels, loadings):
    cells = float(early.shape[1] * math.prod(SIZES))
    turned = loadings.T
    high = lax.reduce_precision(turned, 8, 7)
    low = turned - high
    split = jnp.concatenate([high, low, high, low], 1).astype(bf16)

    late_full = jnp.concatenate([late, late_logs[None], jnp.zeros((7,) + late_logs.shape, bf16)], 0)
    early_all = spread(early, EARLY_GROUP)
    late_own = lax.all_gather(late_full, "z", axis=0, tiled=False)
    late_other = lax.ppermute(late_own, "core", [(0, 1), (1, 0)])
    partial = attention(early_all, late_own, late_other)
    got = exchange(partial, EARLY_GROUP)
    projected, sums = moments(got, early, labels[None])
    sums = jnp.sum(exchange(sums, EARLY_GROUP), 0)
    sums = jnp.sum(spread(sums, LATE_GROUP), 0)
    sums = spread(sums, EARLY_GROUP)
    return projected, correlate(sums, split, cells)


def solution(mesh):
    named = Mesh(mesh.devices.reshape(SIZES), AXES)
    in_specs = (P(None, AXES), P(None, AXES), P(AXES), P(AXES), P())
    out_specs = (P(None, AXES), P())
    return jax.shard_map(
        program, mesh=named, in_specs=in_specs, out_specs=out_specs, check_vma=False
    )
```

```python
import functools
import math

import jax
import jax.numpy as jnp
from jax import lax
from jax.experimental import pallas as pl
from jax.experimental.pallas import tpu as pltpu
from jax.sharding import Mesh
from jax.sharding import PartitionSpec as P


f32 = jnp.float32
bf16 = jnp.bfloat16

DIM = 64
FATES = 256
EPSILON = 1e-06
SHARP = 8.0 / DIM
LOG2E = math.log2(math.e)
LOWEST = -1e30

AXES = ("yl", "z", "yh", "x", "core")
SIZES = (2, 8, 2, 4, 2)
EARLY_GROUP = ("yl", "yh", "x")
LATE_GROUP = ("z", "core")


def split3(v):
    high = v.astype(bf16).astype(f32)
    rest = v - high
    mid = rest.astype(bf16).astype(f32)
    return high, mid, rest - mid


def put_rows(base, row, first, value):
    for k, piece in enumerate(split3(value)):
        base = jnp.where(row == first + k, piece, base)
    return base


def pack_kernel(late_ref, log_ref, one_ref, all_ref):
    cells = late_ref.shape[1]
    blocks = [late_ref[:, 128 * k : 128 * (k + 1)] for k in range(cells // 128)]
    logs = [log_ref[:, 128 * k : 128 * (k + 1)].astype(f32) for k in range(cells // 128)]
    tail = jnp.concatenate(logs + [jnp.zeros((8 - cells // 128, 128), f32)], 0).astype(bf16)
    one = jnp.concatenate(blocks + [tail], 0)
    one_ref[0] = one
    for k in range(all_ref.shape[0]):
        all_ref[k] = one


def pack(late, logs, copies):
    rows = DIM * late.shape[1] // 128 + 8
    return pl.pallas_call(
        pack_kernel,
        out_shape=(
            jax.ShapeDtypeStruct((1, rows, 128), bf16),
            jax.ShapeDtypeStruct((copies, rows, 128), bf16),
        ),
        in_specs=[pl.BlockSpec(memory_space=pltpu.VMEM)] * 2,
        out_specs=(pl.BlockSpec(memory_space=pltpu.VMEM),) * 2,
        compiler_params=pltpu.CompilerParams(vmem_limit_bytes=8 * 2**20),
        name="pack",
    )(late, logs[None])


def attention_kernel(*refs, n_x, n_late, skip, tile, parts, has_state):
    refs = list(refs)
    slot_ref = refs.pop(0)
    x_refs = [refs.pop(0) for _ in range(n_x)]
    late_refs = [refs.pop(0) for _ in range(n_late)]
    if has_state:
        xa, state_ref = x_refs[0], refs.pop(0)
        out_ref = refs.pop(0)
    else:
        out_ref, xa = refs.pop(0), refs.pop(0)
    ya, yw, sbuf, mbuf, acc = refs
    wide = 256
    pairs = xa.shape[0]
    chunk = (late_refs[0].shape[1] - 8) * 2
    groups = chunk // 128
    chunks = sum(r.shape[0] - skip for r in late_refs)
    tiles = chunks * chunk // tile

    if not has_state:
        row = lax.broadcasted_iota(jnp.int32, (DIM, wide), 0)
        blank = jnp.where(row < 3, 1.0, jnp.zeros((DIM, wide), f32))
        per = x_refs[0].shape[0] // 2
        for b in range(pairs):
            ref, k = x_refs[b // per], 2 * (b % per)
            x = jnp.concatenate([ref[k], ref[k + 1]], 1).astype(f32)
            norms = jnp.sum(x * x, 0, keepdims=True)
            high, mid, low = split3(x * (2.0 * SHARP * LOG2E))
            extra = put_rows(blank, row, 3, norms * (-SHARP * LOG2E))
            xa[b] = jnp.concatenate([high, extra, mid, low], 0).astype(bf16)

    def prepare_late(y_ref, b, slot):
        yb = jnp.concatenate([y_ref[b, DIM * k : DIM * (k + 1), :] for k in range(groups)], 1)
        tail = y_ref[b, DIM * groups : DIM * groups + 8, :].astype(f32)
        logs = jnp.concatenate([tail[k : k + 1] for k in range(groups)], 1)
        y = yb.astype(f32)
        bias = (logs - jnp.sum(y * y, 0, keepdims=True) * SHARP) * LOG2E
        row = lax.broadcasted_iota(jnp.int32, (DIM, chunk), 0)
        extra = jnp.where((row >= 3) & (row < 6), 1.0, jnp.zeros((DIM, chunk), f32))
        extra = put_rows(extra, row, 0, bias)
        t = jnp.concatenate([y, extra], 0).T
        lane = lax.broadcasted_iota(jnp.int32, (chunk, 128), 1)
        twice = jnp.where(lane < DIM, t, pltpu.roll(t, DIM, 1))
        first = pl.multiple_of(slot * chunk, chunk)
        ya[pl.ds(first, chunk), :] = jnp.concatenate([t, twice], 1).astype(bf16)
        ones = jnp.where(lax.broadcasted_iota(jnp.int32, (16, chunk), 0) == 0, 1.0, 0.0)
        yw[:, pl.ds(first, chunk)] = jnp.concatenate([yb, ones.astype(bf16)], 0)

    if skip:
        here = slot_ref[2 * pairs]
        count = late_refs[0].shape[0]

        def prepare(j, carry):
            for k, ref in enumerate(late_refs):
                prepare_late(ref, (here + 1 + j) % count, k * (count - 1) + j)
            return carry

        lax.fori_loop(0, count - 1, prepare, 0)
    else:
        for k, ref in enumerate(late_refs):
            prepare_late(ref, 0, k)
    acc[...] = jnp.zeros_like(acc)

    def score_part(pair, first, offset, size, slot, top):
        s = jnp.dot(ya[pl.ds(first + offset, size), :], xa[pair], preferred_element_type=f32)
        sbuf[slot, offset : offset + size, :] = s
        here = jnp.max(s.reshape(size // 8, 8, wide), 0)
        return here if top is None else jnp.maximum(top, here)

    steps = pairs * tiles
    spans = [(sum(parts[:k]), parts[k]) for k in range(len(parts))]
    top = None
    for offset, size in spans:
        top = score_part(0, 0, offset, size, 0, top)
    mbuf[0] = top

    def step(n, slot, before):
        pair = n // tiles
        first = pl.multiple_of((n % tiles) * tile, tile)
        following = jnp.minimum(n + 1, steps - 1)
        next_first = pl.multiple_of((following % tiles) * tile, tile)
        fresh = n % tiles == 0
        left, right = slot_ref[2 * pair], slot_ref[2 * pair + 1]
        carried = acc[...]
        if has_state:
            state = jnp.concatenate([state_ref[left], state_ref[right]], 1)
            before = jnp.where(fresh, state[DIM + 1 : DIM + 2], before)
            carried = jnp.where(fresh, state, carried)
        else:
            before = jnp.where(fresh, LOWEST, before)
        now = jnp.maximum(before, jnp.max(mbuf[slot], 0, keepdims=True))
        shrink = jnp.exp2(before - now)
        top = None
        sums = None
        for offset, size in spans:
            top = score_part(following // tiles, next_first, offset, size, 1 - slot, top)
            weights = jnp.exp2(sbuf[slot, offset : offset + size, :] - now).astype(bf16)
            more = jnp.dot(yw[:, pl.ds(first + offset, size)], weights, preferred_element_type=f32)
            sums = more if sums is None else sums + more
        mbuf[1 - slot] = top
        total = carried * shrink + sums[:72]
        row = lax.broadcasted_iota(jnp.int32, (72, wide), 0)
        packed = jnp.where(row == DIM + 1, now, total)
        acc[...] = packed
        out_ref[left] = packed[:, :128]
        out_ref[right] = packed[:, 128:]
        return now

    def two_steps(i, before):
        return step(2 * i + 1, 1, step(2 * i, 0, before))

    lax.fori_loop(0, steps // 2, two_steps, jnp.full((1, wide), LOWEST, f32))


def attention(slots, early, late, state=None, skip=0, tile=1024, parts=(512, 512)):
    wide = 256
    pairs = early[0].shape[0] if state is not None else sum(e.shape[0] for e in early) // 2
    late_total = sum(r.shape[0] - skip for r in late) * (late[0].shape[1] - 8) * 2
    out_shape = [jax.ShapeDtypeStruct((2 * pairs, 72, 128), f32)]
    operands = list(early) + list(late)
    if state is None:
        out_shape.append(jax.ShapeDtypeStruct((pairs, 256, wide), bf16))
    else:
        operands.append(state)
    vmem = pl.BlockSpec(memory_space=pltpu.VMEM)
    return pl.pallas_call(
        functools.partial(
            attention_kernel,
            n_x=len(early),
            n_late=len(late),
            skip=skip,
            tile=tile,
            parts=parts,
            has_state=state is not None,
        ),
        out_shape=out_shape,
        in_specs=[pl.BlockSpec(memory_space=pltpu.SMEM)] + [vmem] * len(operands),
        out_specs=[vmem] * len(out_shape),
        scratch_shapes=[
            pltpu.VMEM((late_total, 256), bf16),
            pltpu.VMEM((80, late_total), bf16),
            pltpu.VMEM((2, tile, wide), f32),
            pltpu.VMEM((2, 8, wide), f32),
            pltpu.VMEM((72, wide), f32),
        ],
        compiler_params=pltpu.CompilerParams(vmem_limit_bytes=32 * 2**20),
    )(slots, *operands)


def moments_kernel(got_ref, x_ref, label_ref, projected_ref, sums_ref):
    peers, _, cells = got_ref.shape
    top = got_ref[0, DIM : DIM + 8, :][1:2]
    for p in range(1, peers):
        top = jnp.maximum(top, got_ref[p, DIM : DIM + 8, :][1:2])
    total = jnp.zeros((72, cells), f32)
    for p in range(peers):
        block = got_ref[p]
        total = total + block * jnp.exp2(block[DIM + 1 : DIM + 2] - top)
    projected = total[:DIM] / total[DIM : DIM + 1]
    projected_ref[...] = projected
    moved = projected - x_ref[...].astype(f32)
    classes = lax.broadcasted_iota(jnp.int32, (FATES, cells), 0)
    indicator = jnp.where(classes == label_ref[...], 1.0, 0.0)
    across = (((1,), (1,)), ((), ()))
    by_class = lax.dot_general(
        moved, indicator, across, precision=lax.Precision.HIGHEST, preferred_element_type=f32
    )
    padded = jnp.concatenate([moved, jnp.zeros((128 - DIM, cells), f32)], 0)
    second = lax.dot_general(
        moved, padded, across, precision=lax.Precision.HIGHEST, preferred_element_type=f32
    )
    count = jnp.sum(indicator, 1, keepdims=True)
    lane = lax.broadcasted_iota(jnp.int32, (DIM, 128), 1)
    for q in range(FATES // DIM):
        second = jnp.where(lane == DIM + q, count[DIM * q : DIM * (q + 1)], second)
    sums_ref[:8] = by_class.reshape(8, 8, FATES)
    sums_ref[8:] = jnp.concatenate([second, jnp.zeros((DIM, 128), f32)], 1).reshape(8, 8, FATES)


def moments(got, early, labels):
    return pl.pallas_call(
        moments_kernel,
        out_shape=(
            jax.ShapeDtypeStruct(early.shape, f32),
            jax.ShapeDtypeStruct((16, 8, FATES), f32),
        ),
        in_specs=[pl.BlockSpec(memory_space=pltpu.VMEM)] * 3,
        out_specs=(pl.BlockSpec(memory_space=pltpu.VMEM),) * 2,
        compiler_params=pltpu.CompilerParams(vmem_limit_bytes=16 * 2**20),
        name="moments",
    )(got, early, labels)


def correlate_kernel(sums_ref, split_ref, out_ref, right, stage, sems, *, cells, block):
    genes = split_ref.shape[0]
    by_class = sums_ref[:8].reshape(DIM, FATES) / cells
    second = sums_ref[8:].reshape(DIM, FATES)[:, :128]
    flipped = second.T
    share = jnp.concatenate([flipped[DIM + q : DIM + q + 1] for q in range(FATES // DIM)], 1) / cells
    mean = jnp.sum(by_class, 1, keepdims=True)
    mean_row = jnp.broadcast_to(mean, (DIM, 128)).T[:1, :DIM]
    square = second[:, :DIM] / cells - mean * mean_row
    cross = (by_class - mean * share) / jnp.sqrt(share * (1.0 - share))
    both = jnp.concatenate([cross, square, square], 1)
    high = both.astype(bf16)
    low = (both - high.astype(f32)).astype(bf16)
    right[...] = jnp.concatenate([high, high, low, low], 0)

    def copy(k):
        rows = pl.ds(k * block, block)
        return pltpu.make_async_copy(stage.at[rows], out_ref.at[rows], sems.at[k])

    for k in range(genes // block):
        rows = split_ref[k * block : (k + 1) * block]
        product = jnp.dot(rows, right[...], preferred_element_type=f32)
        halves = rows[:, :128].astype(f32)
        variance = jnp.sum(product[:, FATES:] * halves, 1, keepdims=True) + EPSILON
        stage[k * block : (k + 1) * block] = product[:, :FATES] * (1.0 / jnp.sqrt(variance))
        copy(k).start()
    for k in range(genes // block):
        copy(k).wait()


def correlate(sums, split, cells, block=400):
    genes = split.shape[0]
    return pl.pallas_call(
        functools.partial(correlate_kernel, cells=cells, block=block),
        out_shape=jax.ShapeDtypeStruct((genes, FATES), f32),
        in_specs=[pl.BlockSpec(memory_space=pltpu.VMEM)] * 2,
        out_specs=pl.BlockSpec(memory_space=pl.ANY),
        scratch_shapes=[
            pltpu.VMEM((256, FATES + 128), bf16),
            pltpu.VMEM((genes, FATES), f32),
            pltpu.SemaphoreType.DMA((genes // block,)),
        ],
        compiler_params=pltpu.CompilerParams(vmem_limit_bytes=16 * 2**20),
        name="correlate",
    )(sums, split)


def shift(n, k):
    return [(i, (i + k) % n) for i in range(n)]


def shift_y(k):
    place = [y % 2 * 2 + y // 2 for y in range(4)]
    return [(place[y], place[(y + k) % 4]) for y in range(4)]


def exchange(blocks, axes):
    return lax.all_to_all(blocks, axes, 0, 0, tiled=False)


def spread(block, axes):
    return exchange(jnp.broadcast_to(block[None], (16,) + block.shape), axes)


def program(early, late, late_logs, labels, loadings):
    cells = float(early.shape[1] * math.prod(SIZES))
    turned = loadings.T
    high = lax.reduce_precision(turned, 8, 7)
    low = turned - high
    split = jnp.concatenate([high, low, high, low], 1).astype(bf16)

    late_one, late_copies = pack(late, late_logs, SIZES[1])
    late_own = exchange(late_copies, "z")
    swap = [(0, 1), (1, 0)]
    late_near = lax.ppermute(late_one, "core", swap)
    line = [early] + [lax.ppermute(early, "x", shift(4, k)) for k in range(1, 4)]
    line = jnp.stack(line)
    early_all = [line] + [lax.ppermute(line, ("yl", "yh"), shift_y(k)) for k in range(1, 4)]
    y, x = 2 * lax.axis_index("yh") + lax.axis_index("yl"), lax.axis_index("x")
    back = jnp.arange(16, dtype=jnp.int32)
    to_y, to_x = (y - back // 4) % 4, (x - back % 4) % 4
    slots = to_y % 2 * 8 + to_y // 2 * 4 + to_x
    slots = jnp.concatenate([slots, lax.axis_index("z")[None]]).astype(jnp.int32)
    partial, prepared = attention(slots, early_all, [late_one, late_near])
    late_other = lax.ppermute(late_own, "core", swap)
    rest = dict(skip=1, tile=1792, parts=(512, 512, 512, 256))
    (partial,) = attention(slots, [prepared], [late_own], partial, **rest)
    (partial,) = attention(slots, [prepared], [late_other], partial, **rest)
    got = exchange(partial, EARLY_GROUP)
    projected, sums = moments(got, early, labels[None])
    sums = jnp.sum(exchange(sums, EARLY_GROUP), 0)
    sums = jnp.sum(spread(sums, LATE_GROUP), 0)
    sums = spread(sums, EARLY_GROUP)
    return projected, correlate(sums, split, cells)


def solution(mesh):
    named = Mesh(mesh.devices.reshape(SIZES), AXES)
    in_specs = (P(None, AXES), P(None, AXES), P(AXES), P(AXES), P())
    out_specs = (P(None, AXES), P())
    return jax.shard_map(
        program, mesh=named, in_specs=in_specs, out_specs=out_specs, check_vma=False
    )
```

```python
import functools
import math

import jax
import jax.numpy as jnp
from jax import lax
from jax.experimental import pallas as pl
from jax.experimental.pallas import tpu as pltpu
from jax.sharding import Mesh
from jax.sharding import PartitionSpec as P


f32 = jnp.float32
bf16 = jnp.bfloat16

DIM = 64
FATES = 256
EPSILON = 1e-06
SHARP = 8.0 / DIM
LOG2E = math.log2(math.e)
LOWEST = -1e30

AXES = ("yl", "z", "yh", "x", "core")
SIZES = (2, 8, 2, 4, 2)
EARLY_GROUP = ("yl", "yh", "x")
LATE_GROUP = ("z", "core")

Z_STEPS = (1, 7, 2, 6, 3, 5, 4)


def split3(v):
    high = v.astype(bf16).astype(f32)
    rest = v - high
    mid = rest.astype(bf16).astype(f32)
    return high, mid, rest - mid


def put_rows(base, row, first, value):
    for k, piece in enumerate(split3(value)):
        base = jnp.where(row == first + k, piece, base)
    return base


def pack_kernel(late_ref, log_ref, out_ref):
    cells = late_ref.shape[1]
    blocks = [late_ref[:, 128 * k : 128 * (k + 1)] for k in range(cells // 128)]
    logs = [log_ref[:, 128 * k : 128 * (k + 1)].astype(f32) for k in range(cells // 128)]
    tail = jnp.concatenate(logs + [jnp.zeros((8 - cells // 128, 128), f32)], 0).astype(bf16)
    out_ref[0] = jnp.concatenate(blocks + [tail], 0)


def pack(late, logs):
    rows = DIM * late.shape[1] // 128 + 8
    return pl.pallas_call(
        pack_kernel,
        out_shape=jax.ShapeDtypeStruct((1, rows, 128), bf16),
        in_specs=[pl.BlockSpec(memory_space=pltpu.VMEM)] * 2,
        out_specs=pl.BlockSpec(memory_space=pltpu.VMEM),
        compiler_params=pltpu.CompilerParams(vmem_limit_bytes=8 * 2**20),
        name="pack",
    )(late, logs[None])


def attention_kernel(*refs, n_x, n_late, tile, score_parts, parts, has_state):
    refs = list(refs)
    x_refs = [refs.pop(0) for _ in range(n_x)]
    late_refs = [refs.pop(0) for _ in range(n_late)]
    if has_state:
        xa, state_ref = x_refs[0], refs.pop(0)
        out_ref = refs.pop(0)
    else:
        out_ref, xa = refs.pop(0), refs.pop(0)
    ya, yw, sbuf, mbuf, acc = refs
    wide = 256
    pairs = xa.shape[0]
    chunk = (late_refs[0].shape[1] - 8) * 2
    groups = chunk // 128
    tiles = n_late * chunk // tile

    if not has_state:
        row = lax.broadcasted_iota(jnp.int32, (DIM, wide), 0)
        blank = jnp.where(row < 3, 1.0, jnp.zeros((DIM, wide), f32))
        per = x_refs[0].shape[0] // 2
        for b in range(pairs):
            ref, k = x_refs[b // per], 2 * (b % per)
            x = jnp.concatenate([ref[k], ref[k + 1]], 1).astype(f32)
            norms = jnp.sum(x * x, 0, keepdims=True)
            high, mid, low = split3(x * (2.0 * SHARP * LOG2E))
            extra = put_rows(blank, row, 3, norms * (-SHARP * LOG2E))
            xa[b] = jnp.concatenate([high, extra, mid, low], 0).astype(bf16)

    def prepare_late(y_ref, b, slot):
        yb = jnp.concatenate([y_ref[b, DIM * k : DIM * (k + 1), :] for k in range(groups)], 1)
        tail = y_ref[b, DIM * groups : DIM * groups + 8, :].astype(f32)
        logs = jnp.concatenate([tail[k : k + 1] for k in range(groups)], 1)
        y = yb.astype(f32)
        bias = (logs - jnp.sum(y * y, 0, keepdims=True) * SHARP) * LOG2E
        row = lax.broadcasted_iota(jnp.int32, (DIM, chunk), 0)
        extra = jnp.where((row >= 3) & (row < 6), 1.0, jnp.zeros((DIM, chunk), f32))
        extra = put_rows(extra, row, 0, bias)
        t = jnp.concatenate([y, extra], 0).T
        lane = lax.broadcasted_iota(jnp.int32, (chunk, 128), 1)
        twice = jnp.where(lane < DIM, t, pltpu.roll(t, DIM, 1))
        first = pl.multiple_of(slot * chunk, chunk)
        ya[pl.ds(first, chunk), :] = jnp.concatenate([t, twice], 1).astype(bf16)
        ones = jnp.where(lax.broadcasted_iota(jnp.int32, (16, chunk), 0) == 0, 1.0, 0.0)
        yw[:, pl.ds(first, chunk)] = jnp.concatenate([yb, ones.astype(bf16)], 0)

    for k, ref in enumerate(late_refs):
        prepare_late(ref, 0, k)
    acc[...] = jnp.zeros_like(acc)

    def score_part(pair, first, offset, size, slot, top):
        s = jnp.dot(ya[pl.ds(first + offset, size), :], xa[pair], preferred_element_type=f32)
        sbuf[slot, offset : offset + size, :] = s
        here = jnp.max(s.reshape(size // 8, 8, wide), 0)
        return here if top is None else jnp.maximum(top, here)

    steps = pairs * tiles
    spans = [(sum(parts[:k]), parts[k]) for k in range(len(parts))]
    score_spans = [(sum(score_parts[:k]), score_parts[k]) for k in range(len(score_parts))]
    top = None
    for offset, size in score_spans:
        top = score_part(0, 0, offset, size, 0, top)
    mbuf[0] = top

    def step(n, slot, before):
        pair = n // tiles
        first = pl.multiple_of((n % tiles) * tile, tile)
        following = jnp.minimum(n + 1, steps - 1)
        next_first = pl.multiple_of((following % tiles) * tile, tile)
        fresh = n % tiles == 0
        left, right = 2 * pair, 2 * pair + 1
        carried = acc[...]
        if has_state:
            state = jnp.concatenate([state_ref[left], state_ref[right]], 1)
            before = jnp.where(fresh, state[DIM + 1 : DIM + 2], before)
            carried = jnp.where(fresh, state, carried)
        else:
            before = jnp.where(fresh, LOWEST, before)
        now = jnp.maximum(before, jnp.max(mbuf[slot], 0, keepdims=True))
        shrink = jnp.exp2(before - now)
        top = None
        sums = None
        left_over = list(score_spans)
        for offset, size in spans:
            while left_over and left_over[0][0] <= offset:
                span = left_over.pop(0)
                top = score_part(following // tiles, next_first, *span, 1 - slot, top)
            weights = jnp.exp2(sbuf[slot, offset : offset + size, :] - now).astype(bf16)
            more = jnp.dot(yw[:, pl.ds(first + offset, size)], weights, preferred_element_type=f32)
            sums = more if sums is None else sums + more
        mbuf[1 - slot] = top
        total = carried * shrink + sums[:72]
        row = lax.broadcasted_iota(jnp.int32, (72, wide), 0)
        packed = jnp.where(row == DIM + 1, now, total)
        acc[...] = packed
        out_ref[left] = packed[:, :128]
        out_ref[right] = packed[:, 128:]
        return now

    def two_steps(i, before):
        return step(2 * i + 1, 1, step(2 * i, 0, before))

    lax.fori_loop(0, steps // 2, two_steps, jnp.full((1, wide), LOWEST, f32))


def attention(early, late, state=None, tile=1024, score_parts=(512, 512), parts=(512, 512)):
    wide = 256
    pairs = early[0].shape[0] if state is not None else sum(e.shape[0] for e in early) // 2
    late_total = len(late) * (late[0].shape[1] - 8) * 2
    out_shape = [jax.ShapeDtypeStruct((2 * pairs, 72, 128), f32)]
    operands = list(early) + list(late)
    if state is None:
        out_shape.append(jax.ShapeDtypeStruct((pairs, 256, wide), bf16))
    else:
        operands.append(state)
    vmem = pl.BlockSpec(memory_space=pltpu.VMEM)
    return pl.pallas_call(
        functools.partial(
            attention_kernel,
            n_x=len(early),
            n_late=len(late),
            tile=tile,
            score_parts=score_parts,
            parts=parts,
            has_state=state is not None,
        ),
        out_shape=out_shape,
        in_specs=[vmem] * len(operands),
        out_specs=[vmem] * len(out_shape),
        scratch_shapes=[
            pltpu.VMEM((late_total, 256), bf16),
            pltpu.VMEM((80, late_total), bf16),
            pltpu.VMEM((2, tile, wide), f32),
            pltpu.VMEM((2, 8, wide), f32),
            pltpu.VMEM((72, wide), f32),
        ],
        compiler_params=pltpu.CompilerParams(vmem_limit_bytes=32 * 2**20),
    )(*operands)


def moments_kernel(got_ref, x_ref, label_ref, projected_ref, sums_ref):
    peers, _, cells = got_ref.shape
    top = got_ref[0, DIM : DIM + 8, :][1:2]
    for p in range(1, peers):
        top = jnp.maximum(top, got_ref[p, DIM : DIM + 8, :][1:2])
    total = jnp.zeros((72, cells), f32)
    for p in range(peers):
        block = got_ref[p]
        total = total + block * jnp.exp2(block[DIM + 1 : DIM + 2] - top)
    projected = total[:DIM] / total[DIM : DIM + 1]
    projected_ref[...] = projected
    moved = projected - x_ref[...].astype(f32)
    classes = lax.broadcasted_iota(jnp.int32, (FATES, cells), 0)
    indicator = jnp.where(classes == label_ref[...], 1.0, 0.0)
    across = (((1,), (1,)), ((), ()))
    by_class = lax.dot_general(
        moved, indicator, across, precision=lax.Precision.HIGHEST, preferred_element_type=f32
    )
    padded = jnp.concatenate([moved, jnp.zeros((128 - DIM, cells), f32)], 0)
    second = lax.dot_general(
        moved, padded, across, precision=lax.Precision.HIGHEST, preferred_element_type=f32
    )
    count = jnp.sum(indicator, 1, keepdims=True)
    lane = lax.broadcasted_iota(jnp.int32, (DIM, 128), 1)
    for q in range(FATES // DIM):
        second = jnp.where(lane == DIM + q, count[DIM * q : DIM * (q + 1)], second)
    sums_ref[:8] = by_class.reshape(8, 8, FATES)
    sums_ref[8:] = jnp.concatenate([second, jnp.zeros((DIM, 128), f32)], 1).reshape(8, 8, FATES)


def moments(got, early, labels):
    return pl.pallas_call(
        moments_kernel,
        out_shape=(
            jax.ShapeDtypeStruct(early.shape, f32),
            jax.ShapeDtypeStruct((16, 8, FATES), f32),
        ),
        in_specs=[pl.BlockSpec(memory_space=pltpu.VMEM)] * 3,
        out_specs=(pl.BlockSpec(memory_space=pltpu.VMEM),) * 2,
        compiler_params=pltpu.CompilerParams(vmem_limit_bytes=16 * 2**20),
        name="moments",
    )(got, early, labels)


def correlate_kernel(sums_ref, split_ref, out_ref, right, stage, sems, *, cells, block):
    genes = split_ref.shape[0]
    by_class = sums_ref[:8].reshape(DIM, FATES) / cells
    second = sums_ref[8:].reshape(DIM, FATES)[:, :128]
    flipped = second.T
    share = jnp.concatenate([flipped[DIM + q : DIM + q + 1] for q in range(FATES // DIM)], 1) / cells
    mean = jnp.sum(by_class, 1, keepdims=True)
    mean_row = jnp.broadcast_to(mean, (DIM, 128)).T[:1, :DIM]
    square = second[:, :DIM] / cells - mean * mean_row
    cross = (by_class - mean * share) / jnp.sqrt(share * (1.0 - share))
    both = jnp.concatenate([cross, square, square], 1)
    high = both.astype(bf16)
    low = (both - high.astype(f32)).astype(bf16)
    right[...] = jnp.concatenate([high, high, low, low], 0)

    def copy(k):
        rows = pl.ds(k * block, block)
        return pltpu.make_async_copy(stage.at[rows], out_ref.at[rows], sems.at[k])

    for k in range(genes // block):
        rows = split_ref[k * block : (k + 1) * block]
        product = jnp.dot(rows, right[...], preferred_element_type=f32)
        halves = rows[:, :128].astype(f32)
        variance = jnp.sum(product[:, FATES:] * halves, 1, keepdims=True) + EPSILON
        stage[k * block : (k + 1) * block] = product[:, :FATES] * (1.0 / jnp.sqrt(variance))
        copy(k).start()
    for k in range(genes // block):
        copy(k).wait()


def correlate(sums, split, cells, block=400):
    genes = split.shape[0]
    return pl.pallas_call(
        functools.partial(correlate_kernel, cells=cells, block=block),
        out_shape=jax.ShapeDtypeStruct((genes, FATES), f32),
        in_specs=[pl.BlockSpec(memory_space=pltpu.VMEM)] * 2,
        out_specs=pl.BlockSpec(memory_space=pl.ANY),
        scratch_shapes=[
            pltpu.VMEM((256, FATES + 128), bf16),
            pltpu.VMEM((genes, FATES), f32),
            pltpu.SemaphoreType.DMA((genes // block,)),
        ],
        compiler_params=pltpu.CompilerParams(vmem_limit_bytes=16 * 2**20),
        name="correlate",
    )(sums, split)


def shift(n, k):
    return [(i, (i + k) % n) for i in range(n)]


def exchange(blocks, axes):
    return lax.all_to_all(blocks, axes, 0, 0, tiled=False)


def spread(block, axes):
    return exchange(jnp.broadcast_to(block[None], (16,) + block.shape), axes)


def program(early, late, late_logs, labels, loadings):
    cells = float(early.shape[1] * math.prod(SIZES))
    turned = loadings.T
    high = lax.reduce_precision(turned, 8, 7)
    low = turned - high
    split = jnp.concatenate([high, low, high, low], 1).astype(bf16)

    early_all = spread(early, EARLY_GROUP)
    late_one = pack(late, late_logs)
    swap = [(0, 1), (1, 0)]
    late_near = lax.ppermute(late_one, "core", swap)
    late_far = []
    for k in Z_STEPS:
        own = lax.ppermute(late_one, "z", shift(SIZES[1], k))
        late_far += [own, lax.ppermute(own, "core", swap)]
    partial, prepared = attention([early_all], [late_one, late_near])
    (partial,) = attention(
        [prepared], late_far, partial, tile=3584, score_parts=(512,) * 7, parts=(512,) * 7
    )
    got = exchange(partial, EARLY_GROUP)
    projected, sums = moments(got, early, labels[None])
    sums = jnp.sum(exchange(sums, EARLY_GROUP), 0)
    sums = jnp.sum(spread(sums, LATE_GROUP), 0)
    sums = spread(sums, EARLY_GROUP)
    return projected, correlate(sums, split, cells)


def solution(mesh):
    named = Mesh(mesh.devices.reshape(SIZES), AXES)
    in_specs = (P(None, AXES), P(None, AXES), P(AXES), P(AXES), P())
    out_specs = (P(None, AXES), P())
    return jax.shard_map(
        program, mesh=named, in_specs=in_specs, out_specs=out_specs, check_vma=False
    )
```

```python
import functools
import math

import jax
import jax.numpy as jnp
from jax import lax
from jax.experimental import pallas as pl
from jax.experimental.pallas import tpu as pltpu
from jax.sharding import Mesh
from jax.sharding import PartitionSpec as P


f32 = jnp.float32
bf16 = jnp.bfloat16

DIM = 64
FATES = 256
EPSILON = 1e-06
SHARP = 8.0 / DIM
LOG2E = math.log2(math.e)
LOWEST = -1e30

AXES = ("yl", "z", "yh", "x", "core")
SIZES = (2, 8, 2, 4, 2)
EARLY_GROUP = ("yl", "yh", "x")
PLANE = ("yl", "yh", "x", "core")


def split3(v):
    high = v.astype(bf16).astype(f32)
    rest = v - high
    mid = rest.astype(bf16).astype(f32)
    return high, mid, rest - mid


def put_rows(base, row, first, value):
    for k, piece in enumerate(split3(value)):
        base = jnp.where(row == first + k, piece, base)
    return base


def pack_kernel(late_ref, log_ref, all_ref):
    cells = late_ref.shape[1]
    blocks = [late_ref[:, 128 * k : 128 * (k + 1)] for k in range(cells // 128)]
    logs = [log_ref[:, 128 * k : 128 * (k + 1)].astype(f32) for k in range(cells // 128)]
    tail = jnp.concatenate(logs + [jnp.zeros((8 - cells // 128, 128), f32)], 0).astype(bf16)
    one = jnp.concatenate(blocks + [tail], 0)
    for k in range(all_ref.shape[0]):
        all_ref[k] = one


def pack(late, logs, copies):
    rows = DIM * late.shape[1] // 128 + 8
    return pl.pallas_call(
        pack_kernel,
        out_shape=jax.ShapeDtypeStruct((copies, rows, 128), bf16),
        in_specs=[pl.BlockSpec(memory_space=pltpu.VMEM)] * 2,
        out_specs=pl.BlockSpec(memory_space=pltpu.VMEM),
        compiler_params=pltpu.CompilerParams(vmem_limit_bytes=8 * 2**20),
        name="pack",
    )(late, logs[None])


def attention_kernel(*refs, n_x, n_late, tile, score_parts, parts, has_state):
    refs = list(refs)
    slot_ref = refs.pop(0)
    x_refs = [refs.pop(0) for _ in range(n_x)]
    late_refs = [refs.pop(0) for _ in range(n_late)]
    if has_state:
        xa, state_ref = x_refs[0], refs.pop(0)
        out_ref = refs.pop(0)
    else:
        out_ref, xa = refs.pop(0), refs.pop(0)
    ya, yw, sbuf, mbuf, acc = refs
    wide = 256
    pairs = xa.shape[0]
    chunk = (late_refs[0].shape[1] - 8) * 2
    groups = chunk // 128
    tiles = n_late * late_refs[0].shape[0] * chunk // tile

    if not has_state:
        row = lax.broadcasted_iota(jnp.int32, (DIM, wide), 0)
        blank = jnp.where(row < 3, 1.0, jnp.zeros((DIM, wide), f32))
        per = x_refs[0].shape[0] // 2
        for b in range(pairs):
            ref, k = x_refs[b // per], 2 * (b % per)
            x = jnp.concatenate([ref[k], ref[k + 1]], 1).astype(f32)
            norms = jnp.sum(x * x, 0, keepdims=True)
            high, mid, low = split3(x * (2.0 * SHARP * LOG2E))
            extra = put_rows(blank, row, 3, norms * (-SHARP * LOG2E))
            xa[b] = jnp.concatenate([high, extra, mid, low], 0).astype(bf16)

    def prepare_late(y_ref, b, slot):
        yb = jnp.concatenate([y_ref[b, DIM * k : DIM * (k + 1), :] for k in range(groups)], 1)
        tail = y_ref[b, DIM * groups : DIM * groups + 8, :].astype(f32)
        logs = jnp.concatenate([tail[k : k + 1] for k in range(groups)], 1)
        y = yb.astype(f32)
        bias = (logs - jnp.sum(y * y, 0, keepdims=True) * SHARP) * LOG2E
        row = lax.broadcasted_iota(jnp.int32, (DIM, chunk), 0)
        extra = jnp.where((row >= 3) & (row < 6), 1.0, jnp.zeros((DIM, chunk), f32))
        extra = put_rows(extra, row, 0, bias)
        t = jnp.concatenate([y, extra], 0).T
        lane = lax.broadcasted_iota(jnp.int32, (chunk, 128), 1)
        twice = jnp.where(lane < DIM, t, pltpu.roll(t, DIM, 1))
        first = pl.multiple_of(slot * chunk, chunk)
        ya[pl.ds(first, chunk), :] = jnp.concatenate([t, twice], 1).astype(bf16)
        ones = jnp.where(lax.broadcasted_iota(jnp.int32, (16, chunk), 0) == 0, 1.0, 0.0)
        yw[:, pl.ds(first, chunk)] = jnp.concatenate([yb, ones.astype(bf16)], 0)

    for k, ref in enumerate(late_refs):
        for j in range(ref.shape[0]):
            prepare_late(ref, j, k * ref.shape[0] + j)
    acc[...] = jnp.zeros_like(acc)

    def score_part(pair, first, offset, size, slot, top):
        s = jnp.dot(ya[pl.ds(first + offset, size), :], xa[pair], preferred_element_type=f32)
        sbuf[slot, offset : offset + size, :] = s
        here = jnp.max(s.reshape(size // 8, 8, wide), 0)
        return here if top is None else jnp.maximum(top, here)

    steps = pairs * tiles
    spans = [(sum(parts[:k]), parts[k]) for k in range(len(parts))]
    score_spans = [(sum(score_parts[:k]), score_parts[k]) for k in range(len(score_parts))]
    top = None
    for offset, size in score_spans:
        top = score_part(0, 0, offset, size, 0, top)
    mbuf[0] = top

    def step(n, slot, before):
        pair = n // tiles
        first = pl.multiple_of((n % tiles) * tile, tile)
        following = jnp.minimum(n + 1, steps - 1)
        next_first = pl.multiple_of((following % tiles) * tile, tile)
        fresh = n % tiles == 0
        left, right = slot_ref[2 * pair], slot_ref[2 * pair + 1]
        carried = acc[...]
        if has_state:
            state = jnp.concatenate([state_ref[left], state_ref[right]], 1)
            before = jnp.where(fresh, state[DIM + 1 : DIM + 2], before)
            carried = jnp.where(fresh, state, carried)
        else:
            before = jnp.where(fresh, LOWEST, before)
        now = jnp.maximum(before, jnp.max(mbuf[slot], 0, keepdims=True))
        shrink = jnp.exp2(before - now)
        top = None
        sums = None
        left_over = list(score_spans)
        for offset, size in spans:
            while left_over and left_over[0][0] <= offset:
                span = left_over.pop(0)
                top = score_part(following // tiles, next_first, *span, 1 - slot, top)
            weights = jnp.exp2(sbuf[slot, offset : offset + size, :] - now).astype(bf16)
            more = jnp.dot(yw[:, pl.ds(first + offset, size)], weights, preferred_element_type=f32)
            sums = more if sums is None else sums + more
        mbuf[1 - slot] = top
        total = carried * shrink + sums[:72]
        row = lax.broadcasted_iota(jnp.int32, (72, wide), 0)
        packed = jnp.where(row == DIM + 1, now, total)
        acc[...] = packed
        out_ref[left] = packed[:, :128]
        out_ref[right] = packed[:, 128:]
        return now

    def two_steps(i, before):
        return step(2 * i + 1, 1, step(2 * i, 0, before))

    lax.fori_loop(0, steps // 2, two_steps, jnp.full((1, wide), LOWEST, f32))


def attention(slots, early, late, state=None, tile=1024, score_parts=(512, 512), parts=(512, 512)):
    wide = 256
    pairs = early[0].shape[0] if state is not None else sum(e.shape[0] for e in early) // 2
    late_total = len(late) * late[0].shape[0] * (late[0].shape[1] - 8) * 2
    out_shape = [jax.ShapeDtypeStruct((2 * pairs, 72, 128), f32)]
    operands = list(early) + list(late)
    if state is None:
        out_shape.append(jax.ShapeDtypeStruct((pairs, 256, wide), bf16))
    else:
        operands.append(state)
    vmem = pl.BlockSpec(memory_space=pltpu.VMEM)
    return pl.pallas_call(
        functools.partial(
            attention_kernel,
            n_x=len(early),
            n_late=len(late),
            tile=tile,
            score_parts=score_parts,
            parts=parts,
            has_state=state is not None,
        ),
        out_shape=out_shape,
        in_specs=[pl.BlockSpec(memory_space=pltpu.SMEM)] + [vmem] * len(operands),
        out_specs=[vmem] * len(out_shape),
        scratch_shapes=[
            pltpu.VMEM((late_total, 256), bf16),
            pltpu.VMEM((80, late_total), bf16),
            pltpu.VMEM((2, tile, wide), f32),
            pltpu.VMEM((2, 8, wide), f32),
            pltpu.VMEM((72, wide), f32),
        ],
        compiler_params=pltpu.CompilerParams(vmem_limit_bytes=32 * 2**20),
    )(slots, *operands)


def moments_kernel(got_ref, x_ref, label_ref, projected_ref, sums_ref):
    peers, _, cells = got_ref.shape
    top = got_ref[0, DIM : DIM + 8, :][1:2]
    for p in range(1, peers):
        top = jnp.maximum(top, got_ref[p, DIM : DIM + 8, :][1:2])
    total = jnp.zeros((72, cells), f32)
    for p in range(peers):
        block = got_ref[p]
        total = total + block * jnp.exp2(block[DIM + 1 : DIM + 2] - top)
    projected = total[:DIM] / total[DIM : DIM + 1]
    projected_ref[...] = projected
    moved = projected - x_ref[...].astype(f32)
    classes = lax.broadcasted_iota(jnp.int32, (FATES, cells), 0)
    indicator = jnp.where(classes == label_ref[...], 1.0, 0.0)
    across = (((1,), (1,)), ((), ()))
    by_class = lax.dot_general(
        moved, indicator, across, precision=lax.Precision.HIGHEST, preferred_element_type=f32
    )
    padded = jnp.concatenate([moved, jnp.zeros((128 - DIM, cells), f32)], 0)
    second = lax.dot_general(
        moved, padded, across, precision=lax.Precision.HIGHEST, preferred_element_type=f32
    )
    count = jnp.sum(indicator, 1, keepdims=True)
    lane = lax.broadcasted_iota(jnp.int32, (DIM, 128), 1)
    for q in range(FATES // DIM):
        second = jnp.where(lane == DIM + q, count[DIM * q : DIM * (q + 1)], second)
    sums_ref[:8] = by_class[:, :128].reshape(8, 8, 128)
    sums_ref[8:16] = by_class[:, 128:].reshape(8, 8, 128)
    sums_ref[16:24] = second.reshape(8, 8, 128)
    sums_ref[24:] = jnp.zeros((8, 8, 128), f32)


def moments(got, early, labels):
    return pl.pallas_call(
        moments_kernel,
        out_shape=(
            jax.ShapeDtypeStruct(early.shape, f32),
            jax.ShapeDtypeStruct((32, 8, 128), f32),
        ),
        in_specs=[pl.BlockSpec(memory_space=pltpu.VMEM)] * 3,
        out_specs=(pl.BlockSpec(memory_space=pltpu.VMEM),) * 2,
        compiler_params=pltpu.CompilerParams(vmem_limit_bytes=16 * 2**20),
        name="moments",
    )(got, early, labels)


def correlate_kernel(sums_ref, split_ref, out_ref, right, stage, sems, *, cells, block):
    genes = split_ref.shape[0]
    halves = [sums_ref[8 * h : 8 * h + 8].reshape(DIM, 128) for h in range(3)]
    by_class = jnp.concatenate(halves[:2], 1) / cells
    second = halves[2]
    flipped = second.T
    share = jnp.concatenate([flipped[DIM + q : DIM + q + 1] for q in range(FATES // DIM)], 1) / cells
    mean = jnp.sum(by_class, 1, keepdims=True)
    mean_row = jnp.broadcast_to(mean, (DIM, 128)).T[:1, :DIM]
    square = second[:, :DIM] / cells - mean * mean_row
    cross = (by_class - mean * share) / jnp.sqrt(share * (1.0 - share))
    both = jnp.concatenate([cross, square, square], 1)
    high = both.astype(bf16)
    low = (both - high.astype(f32)).astype(bf16)
    right[...] = jnp.concatenate([high, high, low, low], 0)

    def copy(k):
        rows = pl.ds(k * block, block)
        return pltpu.make_async_copy(stage.at[rows], out_ref.at[rows], sems.at[k])

    for k in range(genes // block):
        rows = split_ref[k * block : (k + 1) * block]
        product = jnp.dot(rows, right[...], preferred_element_type=f32)
        halves = rows[:, :128].astype(f32)
        variance = jnp.sum(product[:, FATES:] * halves, 1, keepdims=True) + EPSILON
        stage[k * block : (k + 1) * block] = product[:, :FATES] * (1.0 / jnp.sqrt(variance))
        copy(k).start()
    for k in range(genes // block):
        copy(k).wait()


def correlate(sums, split, cells, block=400):
    genes = split.shape[0]
    return pl.pallas_call(
        functools.partial(correlate_kernel, cells=cells, block=block),
        out_shape=jax.ShapeDtypeStruct((genes, FATES), f32),
        in_specs=[pl.BlockSpec(memory_space=pltpu.VMEM)] * 2,
        out_specs=pl.BlockSpec(memory_space=pl.ANY),
        scratch_shapes=[
            pltpu.VMEM((256, FATES + 128), bf16),
            pltpu.VMEM((genes, FATES), f32),
            pltpu.SemaphoreType.DMA((genes // block,)),
        ],
        compiler_params=pltpu.CompilerParams(vmem_limit_bytes=16 * 2**20),
        name="correlate",
    )(sums, split)


def shift(n, k):
    return [(i, (i + k) % n) for i in range(n)]


def shift_y(k):
    place = [y % 2 * 2 + y // 2 for y in range(4)]
    return [(place[y], place[(y + k) % 4]) for y in range(4)]


def exchange(blocks, axes):
    return lax.all_to_all(blocks, axes, 0, 0, tiled=False)


def spread(block, axes, size):
    return exchange(jnp.broadcast_to(block[None], (size,) + block.shape), axes)


def program(early, late, late_logs, labels, loadings):
    cells = float(early.shape[1] * math.prod(SIZES))
    turned = loadings.T
    high = lax.reduce_precision(turned, 8, 7)
    low = turned - high
    split = jnp.concatenate([high, low, high, low], 1).astype(bf16)

    late_copies = pack(late, late_logs, SIZES[1])
    late_own = exchange(late_copies, "z")
    late_other = lax.ppermute(late_own, "core", [(0, 1), (1, 0)])
    line = [early] + [lax.ppermute(early, "x", shift(4, k)) for k in range(1, 4)]
    line = jnp.stack(line)
    turns = [lax.ppermute(line, ("yl", "yh"), shift_y(k)) for k in range(1, 4)]
    y, x = 2 * lax.axis_index("yh") + lax.axis_index("yl"), lax.axis_index("x")
    back = jnp.arange(16, dtype=jnp.int32)
    to_y, to_x = (y - back // 4) % 4, (x - back % 4) % 4
    slots = (to_y % 2 * 8 + to_y // 2 * 4 + to_x).astype(jnp.int32)
    parts = (512,) * 8
    partial, _ = attention(
        slots, [line] + turns, [late_own, late_other], tile=4096, score_parts=parts, parts=parts
    )
    got = exchange(partial, EARLY_GROUP)
    projected, sums = moments(got, early, labels[None])
    sums = jnp.sum(exchange(sums, PLANE), 0)
    sums = jnp.sum(spread(sums, "z", SIZES[1]), 0)
    sums = spread(sums, PLANE, 32)
    return projected, correlate(sums, split, cells)


def solution(mesh):
    named = Mesh(mesh.devices.reshape(SIZES), AXES)
    in_specs = (P(None, AXES), P(None, AXES), P(AXES), P(AXES), P())
    out_specs = (P(None, AXES), P())
    return jax.shard_map(
        program, mesh=named, in_specs=in_specs, out_specs=out_specs, check_vma=False
    )
```

```python
import functools
import math

import jax
import jax.numpy as jnp
from jax import lax
from jax.experimental import pallas as pl
from jax.experimental.pallas import tpu as pltpu
from jax.sharding import Mesh
from jax.sharding import PartitionSpec as P


f32 = jnp.float32
bf16 = jnp.bfloat16

DIM = 64
FATES = 256
EPSILON = 1e-06
SHARP = 8.0 / DIM
LOG2E = math.log2(math.e)
LOWEST = -1e30

AXES = ("yl", "z", "yh", "x", "core")
SIZES = (2, 8, 2, 4, 2)
PLANE = ("yl", "yh", "x", "core")

LINE_ORDER = (2, 1, 3, 0)


def split3(v):
    high = v.astype(bf16).astype(f32)
    rest = v - high
    mid = rest.astype(bf16).astype(f32)
    return high, mid, rest - mid


def put_rows(base, row, first, value):
    for k, piece in enumerate(split3(value)):
        base = jnp.where(row == first + k, piece, base)
    return base


def pack_kernel(late_ref, log_ref, all_ref):
    cells = late_ref.shape[1]
    blocks = [late_ref[:, 128 * k : 128 * (k + 1)] for k in range(cells // 128)]
    logs = [log_ref[:, 128 * k : 128 * (k + 1)].astype(f32) for k in range(cells // 128)]
    tail = jnp.concatenate(logs + [jnp.zeros((8 - cells // 128, 128), f32)], 0).astype(bf16)
    one = jnp.concatenate(blocks + [tail], 0)
    for k in range(all_ref.shape[0]):
        all_ref[k] = one


def pack(late, logs, copies):
    rows = DIM * late.shape[1] // 128 + 8
    return pl.pallas_call(
        pack_kernel,
        out_shape=jax.ShapeDtypeStruct((copies, rows, 128), bf16),
        in_specs=[pl.BlockSpec(memory_space=pltpu.VMEM)] * 2,
        out_specs=pl.BlockSpec(memory_space=pltpu.VMEM),
        compiler_params=pltpu.CompilerParams(vmem_limit_bytes=8 * 2**20),
        name="pack",
    )(late, logs[None])


def ready_kernel(late_ref, ya_ref, yw_ref):
    chunk = (late_ref.shape[1] - 8) * 2
    groups = chunk // 128
    row = lax.broadcasted_iota(jnp.int32, (DIM, chunk), 0)
    lane = lax.broadcasted_iota(jnp.int32, (chunk, 128), 1)
    blank = jnp.where((row >= 3) & (row < 6), 1.0, jnp.zeros((DIM, chunk), f32))
    ones = jnp.where(lax.broadcasted_iota(jnp.int32, (16, chunk), 0) == 0, 1.0, 0.0).astype(bf16)
    for b in range(late_ref.shape[0]):
        yb = jnp.concatenate([late_ref[b, DIM * k : DIM * (k + 1), :] for k in range(groups)], 1)
        tail = late_ref[b, DIM * groups : DIM * groups + 8, :].astype(f32)
        logs = jnp.concatenate([tail[k : k + 1] for k in range(groups)], 1)
        y = yb.astype(f32)
        bias = (logs - jnp.sum(y * y, 0, keepdims=True) * SHARP) * LOG2E
        t = jnp.concatenate([y, put_rows(blank, row, 0, bias)], 0).T
        twice = jnp.where(lane < DIM, t, pltpu.roll(t, DIM, 1))
        ya_ref[b * chunk : (b + 1) * chunk, :] = jnp.concatenate([t, twice], 1).astype(bf16)
        yw_ref[:, b * chunk : (b + 1) * chunk] = jnp.concatenate([yb, ones], 0)


def ready(late):
    total = late.shape[0] * (late.shape[1] - 8) * 2
    return pl.pallas_call(
        ready_kernel,
        out_shape=(
            jax.ShapeDtypeStruct((total, 256), bf16),
            jax.ShapeDtypeStruct((80, total), bf16),
        ),
        in_specs=[pl.BlockSpec(memory_space=pltpu.VMEM)],
        out_specs=(pl.BlockSpec(memory_space=pltpu.VMEM),) * 2,
        compiler_params=pltpu.CompilerParams(vmem_limit_bytes=16 * 2**20),
    )(late)


def line_kernel(x_ref, ya0, yw0, ya1, yw1, out_ref, xa, sbuf, mbuf, acc, *, tile, sub):
    wide = 256
    pairs = x_ref.shape[0] // 2
    halves = ((ya0, yw0), (ya1, yw1))
    per_half = ya0.shape[0] // tile
    row = lax.broadcasted_iota(jnp.int32, (DIM, wide), 0)
    blank = jnp.where(row < 3, 1.0, jnp.zeros((DIM, wide), f32))
    for b in range(pairs):
        x = jnp.concatenate([x_ref[2 * b], x_ref[2 * b + 1]], 1).astype(f32)
        norms = jnp.sum(x * x, 0, keepdims=True)
        high, mid, low = split3(x * (2.0 * SHARP * LOG2E))
        extra = put_rows(blank, row, 3, norms * (-SHARP * LOG2E))
        xa[b] = jnp.concatenate([high, extra, mid, low], 0).astype(bf16)

    offsets = range(0, tile, sub)

    def score_part(i, half, offset, top):
        first = pl.multiple_of(i % per_half * tile, tile)
        rows = halves[half][0][pl.ds(first + offset, sub), :]
        s = jnp.dot(rows, xa[i // per_half], preferred_element_type=f32)
        sbuf[half, offset : offset + sub, :] = s
        here = jnp.max(s.reshape(sub // 8, 8, wide), 0)
        return here if top is None else jnp.maximum(top, here)

    def step(i, half, before, last):
        first = pl.multiple_of(i % per_half * tile, tile)
        now = jnp.max(mbuf[half], 0, keepdims=True)
        if half == 0:
            before = jnp.where(i % per_half == 0, LOWEST, before)
        now = jnp.maximum(before, now)
        top = None
        sums = None
        for offset in offsets:
            if not last:
                top = score_part(i + half, 1 - half, offset, top)
            weights = jnp.exp2(sbuf[half, offset : offset + sub, :] - now).astype(bf16)
            columns = halves[half][1][:, pl.ds(first + offset, sub)]
            more = jnp.dot(columns, weights, preferred_element_type=f32)
            sums = more if sums is None else sums + more
        if not last:
            mbuf[1 - half] = top
        total = acc[...] * jnp.exp2(before - now) + sums[:72]
        acc[...] = total
        if half == 1:
            b = i // per_half
            where = lax.broadcasted_iota(jnp.int32, (72, wide), 0)
            packed = jnp.where(where == DIM + 1, now, total)
            out_ref[2 * b] = packed[:, :128]
            out_ref[2 * b + 1] = packed[:, 128:]
        return now

    acc[...] = jnp.zeros_like(acc)
    top = None
    for offset in offsets:
        top = score_part(0, 0, offset, top)
    mbuf[0] = top

    def two_steps(i, before):
        return step(i, 1, step(i, 0, before, False), False)

    rounds = pairs * per_half
    before = lax.fori_loop(0, rounds - 1, two_steps, jnp.full((1, wide), LOWEST, f32))
    step(rounds - 1, 1, step(rounds - 1, 0, before, False), True)


def attend_line(line, own, other, tile=2048, sub=512):
    return pl.pallas_call(
        functools.partial(line_kernel, tile=tile, sub=sub),
        out_shape=jax.ShapeDtypeStruct((line.shape[0], 72, 128), f32),
        in_specs=[pl.BlockSpec(memory_space=pltpu.VMEM)] * 5,
        out_specs=pl.BlockSpec(memory_space=pltpu.VMEM),
        scratch_shapes=[
            pltpu.VMEM((line.shape[0] // 2, 256, 256), bf16),
            pltpu.VMEM((2, tile, 256), f32),
            pltpu.VMEM((2, 8, 256), f32),
            pltpu.VMEM((72, 256), f32),
        ],
        compiler_params=pltpu.CompilerParams(vmem_limit_bytes=24 * 2**20),
    )(line, *own, *other)


def combine_kernel(slot_ref, *refs):
    out_ref = refs[-1]
    parts = refs[:-1]
    row = lax.broadcasted_iota(jnp.int32, (72, 128), 0)
    for k in range(out_ref.shape[0]):
        blocks = [p[k] for p in parts]
        tops = [b[DIM + 1 : DIM + 2] for b in blocks]
        top = functools.reduce(jnp.maximum, tops)
        total = sum(b * jnp.exp2(t - top) for b, t in zip(blocks, tops))
        out_ref[slot_ref[k]] = jnp.where(row == DIM + 1, top, total)


def combine(slots, parts):
    vmem = pl.BlockSpec(memory_space=pltpu.VMEM)
    return pl.pallas_call(
        combine_kernel,
        out_shape=jax.ShapeDtypeStruct(parts[0].shape, f32),
        in_specs=[pl.BlockSpec(memory_space=pltpu.SMEM)] + [vmem] * len(parts),
        out_specs=vmem,
        compiler_params=pltpu.CompilerParams(vmem_limit_bytes=8 * 2**20),
        name="combine",
    )(slots, *parts)


def moments_kernel(got_ref, x_ref, label_ref, projected_ref, sums_ref):
    peers, _, cells = got_ref.shape
    top = got_ref[0, DIM : DIM + 8, :][1:2]
    for p in range(1, peers):
        top = jnp.maximum(top, got_ref[p, DIM : DIM + 8, :][1:2])
    total = jnp.zeros((72, cells), f32)
    for p in range(peers):
        block = got_ref[p]
        total = total + block * jnp.exp2(block[DIM + 1 : DIM + 2] - top)
    projected = total[:DIM] / total[DIM : DIM + 1]
    projected_ref[...] = projected
    moved = projected - x_ref[...].astype(f32)
    classes = lax.broadcasted_iota(jnp.int32, (FATES, cells), 0)
    indicator = jnp.where(classes == label_ref[...], 1.0, 0.0)
    across = (((1,), (1,)), ((), ()))
    by_class = lax.dot_general(
        moved, indicator, across, precision=lax.Precision.HIGHEST, preferred_element_type=f32
    )
    padded = jnp.concatenate([moved, jnp.zeros((128 - DIM, cells), f32)], 0)
    second = lax.dot_general(
        moved, padded, across, precision=lax.Precision.HIGHEST, preferred_element_type=f32
    )
    count = jnp.sum(indicator, 1, keepdims=True)
    lane = lax.broadcasted_iota(jnp.int32, (DIM, 128), 1)
    for q in range(FATES // DIM):
        second = jnp.where(lane == DIM + q, count[DIM * q : DIM * (q + 1)], second)
    sums_ref[:8] = by_class[:, :128].reshape(8, 8, 128)
    sums_ref[8:16] = by_class[:, 128:].reshape(8, 8, 128)
    sums_ref[16:24] = second.reshape(8, 8, 128)
    sums_ref[24:] = jnp.zeros((8, 8, 128), f32)


def moments(got, early, labels):
    return pl.pallas_call(
        moments_kernel,
        out_shape=(
            jax.ShapeDtypeStruct(early.shape, f32),
            jax.ShapeDtypeStruct((32, 8, 128), f32),
        ),
        in_specs=[pl.BlockSpec(memory_space=pltpu.VMEM)] * 3,
        out_specs=(pl.BlockSpec(memory_space=pltpu.VMEM),) * 2,
        compiler_params=pltpu.CompilerParams(vmem_limit_bytes=16 * 2**20),
        name="moments",
    )(got, early, labels)


def correlate_kernel(sums_ref, split_ref, out_ref, right, stage, sems, *, cells, block):
    genes = split_ref.shape[0]
    halves = [sums_ref[8 * h : 8 * h + 8].reshape(DIM, 128) for h in range(3)]
    by_class = jnp.concatenate(halves[:2], 1) / cells
    second = halves[2]
    flipped = second.T
    share = jnp.concatenate([flipped[DIM + q : DIM + q + 1] for q in range(FATES // DIM)], 1) / cells
    mean = jnp.sum(by_class, 1, keepdims=True)
    mean_row = jnp.broadcast_to(mean, (DIM, 128)).T[:1, :DIM]
    square = second[:, :DIM] / cells - mean * mean_row
    cross = (by_class - mean * share) / jnp.sqrt(share * (1.0 - share))
    both = jnp.concatenate([cross, square, square], 1)
    high = both.astype(bf16)
    low = (both - high.astype(f32)).astype(bf16)
    right[...] = jnp.concatenate([high, high, low, low], 0)

    def copy(k):
        rows = pl.ds(k * block, block)
        return pltpu.make_async_copy(stage.at[rows], out_ref.at[rows], sems.at[k])

    for k in range(genes // block):
        rows = split_ref[k * block : (k + 1) * block]
        product = jnp.dot(rows, right[...], preferred_element_type=f32)
        halves = rows[:, :128].astype(f32)
        variance = jnp.sum(product[:, FATES:] * halves, 1, keepdims=True) + EPSILON
        stage[k * block : (k + 1) * block] = product[:, :FATES] * (1.0 / jnp.sqrt(variance))
        copy(k).start()
    for k in range(genes // block):
        copy(k).wait()


def correlate(sums, split, cells, block=400):
    genes = split.shape[0]
    return pl.pallas_call(
        functools.partial(correlate_kernel, cells=cells, block=block),
        out_shape=jax.ShapeDtypeStruct((genes, FATES), f32),
        in_specs=[pl.BlockSpec(memory_space=pltpu.VMEM)] * 2,
        out_specs=pl.BlockSpec(memory_space=pl.ANY),
        scratch_shapes=[
            pltpu.VMEM((256, FATES + 128), bf16),
            pltpu.VMEM((genes, FATES), f32),
            pltpu.SemaphoreType.DMA((genes // block,)),
        ],
        compiler_params=pltpu.CompilerParams(vmem_limit_bytes=16 * 2**20),
        name="correlate",
    )(sums, split)


def shift(n, k):
    return [(i, (i + k) % n) for i in range(n)]


def shift_y(k):
    place = [y % 2 * 2 + y // 2 for y in range(4)]
    return [(place[y], place[(y + k) % 4]) for y in range(4)]


def exchange(blocks, axes):
    return lax.all_to_all(blocks, axes, 0, 0, tiled=False)


def spread(block, axes, size):
    return exchange(jnp.broadcast_to(block[None], (size,) + block.shape), axes)


def program(early, late, late_logs, labels, loadings):
    cells = float(early.shape[1] * math.prod(SIZES))
    turned = loadings.T
    high = lax.reduce_precision(turned, 8, 7)
    low = turned - high
    split = jnp.concatenate([high, low, high, low], 1).astype(bf16)

    swap = [(0, 1), (1, 0)]
    late_copies = pack(late, late_logs, SIZES[1])
    late_own = exchange(late_copies, "z")
    late_other = lax.ppermute(late_own, "core", swap)
    line = [early] + [lax.ppermute(early, "x", shift(4, k)) for k in range(1, 4)]
    line = jnp.stack(line)
    turns = [lax.ppermute(line, ("yl", "yh"), shift_y(k)) for k in range(1, 4)]
    back = jnp.arange(4, dtype=jnp.int32)
    slots = ((lax.axis_index("x") - back) % 4).astype(jnp.int32)
    own = ready(late_own)
    other = ready(late_other)
    lines = [line] + turns
    parts = {}
    for k in LINE_ORDER:
        parts[k] = attend_line(lines[k], own, other)
        if k:
            parts[k] = lax.ppermute(parts[k], ("yl", "yh"), shift_y(4 - k))
    got = exchange(combine(slots, [parts[k] for k in range(4)]), "x")
    projected, sums = moments(got, early, labels[None])
    sums = jnp.sum(exchange(sums, PLANE), 0)
    sums = jnp.sum(spread(sums, "z", SIZES[1]), 0)
    sums = spread(sums, PLANE, 32)
    return projected, correlate(sums, split, cells)


def solution(mesh):
    named = Mesh(mesh.devices.reshape(SIZES), AXES)
    in_specs = (P(None, AXES), P(None, AXES), P(AXES), P(AXES), P())
    out_specs = (P(None, AXES), P())
    return jax.shard_map(
        program, mesh=named, in_specs=in_specs, out_specs=out_specs, check_vma=False
    )
```

```python
import functools
import math

import jax
import jax.numpy as jnp
from jax import lax
from jax.experimental import pallas as pl
from jax.experimental.pallas import tpu as pltpu
from jax.sharding import Mesh
from jax.sharding import PartitionSpec as P


f32 = jnp.float32
bf16 = jnp.bfloat16

DIM = 64
FATES = 256
EPSILON = 1e-06
SHARP = 8.0 / DIM
LOG2E = math.log2(math.e)
LOWEST = -1e30

AXES = ("yl", "z", "yh", "x", "core")
SIZES = (2, 8, 2, 4, 2)
PLANE = ("yl", "yh", "x")

LINE_ORDER = (2, 1, 3, 0)


def split3(v):
    high = v.astype(bf16).astype(f32)
    rest = v - high
    mid = rest.astype(bf16).astype(f32)
    return high, mid, rest - mid


def put_rows(base, row, first, value):
    for k, piece in enumerate(split3(value)):
        base = jnp.where(row == first + k, piece, base)
    return base


def pack_kernel(late_ref, log_ref, all_ref):
    cells = late_ref.shape[1]
    blocks = [late_ref[:, 128 * k : 128 * (k + 1)] for k in range(cells // 128)]
    logs = [log_ref[:, 128 * k : 128 * (k + 1)].astype(f32) for k in range(cells // 128)]
    tail = jnp.concatenate(logs + [jnp.zeros((8 - cells // 128, 128), f32)], 0).astype(bf16)
    one = jnp.concatenate(blocks + [tail], 0)
    for k in range(all_ref.shape[0]):
        all_ref[k] = one


def pack(late, logs, copies):
    rows = DIM * late.shape[1] // 128 + 8
    return pl.pallas_call(
        pack_kernel,
        out_shape=jax.ShapeDtypeStruct((copies, rows, 128), bf16),
        in_specs=[pl.BlockSpec(memory_space=pltpu.VMEM)] * 2,
        out_specs=pl.BlockSpec(memory_space=pltpu.VMEM),
        compiler_params=pltpu.CompilerParams(vmem_limit_bytes=8 * 2**20),
        name="pack",
    )(late, logs[None])


def ready_kernel(late_ref, ya_ref, yw_ref):
    chunk = (late_ref.shape[1] - 8) * 2
    groups = chunk // 128
    row = lax.broadcasted_iota(jnp.int32, (DIM, chunk), 0)
    lane = lax.broadcasted_iota(jnp.int32, (chunk, 128), 1)
    blank = jnp.where((row >= 3) & (row < 6), 1.0, jnp.zeros((DIM, chunk), f32))
    ones = jnp.where(lax.broadcasted_iota(jnp.int32, (16, chunk), 0) == 0, 1.0, 0.0).astype(bf16)
    for b in range(late_ref.shape[0]):
        yb = jnp.concatenate([late_ref[b, DIM * k : DIM * (k + 1), :] for k in range(groups)], 1)
        tail = late_ref[b, DIM * groups : DIM * groups + 8, :].astype(f32)
        logs = jnp.concatenate([tail[k : k + 1] for k in range(groups)], 1)
        y = yb.astype(f32)
        bias = (logs - jnp.sum(y * y, 0, keepdims=True) * SHARP) * LOG2E
        t = jnp.concatenate([y, put_rows(blank, row, 0, bias)], 0).T
        twice = jnp.where(lane < DIM, t, pltpu.roll(t, DIM, 1))
        ya_ref[b * chunk : (b + 1) * chunk, :] = jnp.concatenate([t, twice], 1).astype(bf16)
        yw_ref[:, b * chunk : (b + 1) * chunk] = jnp.concatenate([yb, ones], 0)


def ready(late):
    total = late.shape[0] * (late.shape[1] - 8) * 2
    return pl.pallas_call(
        ready_kernel,
        out_shape=(
            jax.ShapeDtypeStruct((total, 256), bf16),
            jax.ShapeDtypeStruct((80, total), bf16),
        ),
        in_specs=[pl.BlockSpec(memory_space=pltpu.VMEM)],
        out_specs=(pl.BlockSpec(memory_space=pltpu.VMEM),) * 2,
        compiler_params=pltpu.CompilerParams(vmem_limit_bytes=16 * 2**20),
    )(late)


def line_kernel(x_ref, ya0, yw0, ya1, yw1, out_ref, xa, sbuf, mbuf, acc, *, tile, sub):
    wide = 256
    pairs = x_ref.shape[0] // 2
    halves = ((ya0, yw0), (ya1, yw1))
    per_half = ya0.shape[0] // tile
    row = lax.broadcasted_iota(jnp.int32, (DIM, wide), 0)
    blank = jnp.where(row < 3, 1.0, jnp.zeros((DIM, wide), f32))
    for b in range(pairs):
        x = jnp.concatenate([x_ref[2 * b], x_ref[2 * b + 1]], 1).astype(f32)
        norms = jnp.sum(x * x, 0, keepdims=True)
        high, mid, low = split3(x * (2.0 * SHARP * LOG2E))
        extra = put_rows(blank, row, 3, norms * (-SHARP * LOG2E))
        xa[b] = jnp.concatenate([high, extra, mid, low], 0).astype(bf16)

    offsets = range(0, tile, sub)

    def score_part(i, half, offset, top):
        first = pl.multiple_of(i % per_half * tile, tile)
        rows = halves[half][0][pl.ds(first + offset, sub), :]
        s = jnp.dot(rows, xa[i // per_half], preferred_element_type=f32)
        sbuf[half, offset : offset + sub, :] = s
        here = jnp.max(s.reshape(sub // 8, 8, wide), 0)
        return here if top is None else jnp.maximum(top, here)

    def step(i, half, before, last):
        first = pl.multiple_of(i % per_half * tile, tile)
        now = jnp.max(mbuf[half], 0, keepdims=True)
        if half == 0:
            before = jnp.where(i % per_half == 0, LOWEST, before)
        now = jnp.maximum(before, now)
        top = None
        sums = None
        for offset in offsets:
            if not last:
                top = score_part(i + half, 1 - half, offset, top)
            weights = jnp.exp2(sbuf[half, offset : offset + sub, :] - now).astype(bf16)
            columns = halves[half][1][:, pl.ds(first + offset, sub)]
            more = jnp.dot(columns, weights, preferred_element_type=f32)
            sums = more if sums is None else sums + more
        if not last:
            mbuf[1 - half] = top
        total = acc[...] * jnp.exp2(before - now) + sums[:72]
        acc[...] = total
        if half == 1:
            b = i // per_half
            where = lax.broadcasted_iota(jnp.int32, (72, wide), 0)
            packed = jnp.where(where == DIM + 1, now, total)
            out_ref[2 * b] = packed[:, :128]
            out_ref[2 * b + 1] = packed[:, 128:]
        return now

    acc[...] = jnp.zeros_like(acc)
    top = None
    for offset in offsets:
        top = score_part(0, 0, offset, top)
    mbuf[0] = top

    def two_steps(i, before):
        return step(i, 1, step(i, 0, before, False), False)

    rounds = pairs * per_half
    before = lax.fori_loop(0, rounds - 1, two_steps, jnp.full((1, wide), LOWEST, f32))
    step(rounds - 1, 1, step(rounds - 1, 0, before, False), True)


def attend_line(line, own, other, tile=2048, sub=512):
    return pl.pallas_call(
        functools.partial(line_kernel, tile=tile, sub=sub),
        out_shape=jax.ShapeDtypeStruct((line.shape[0], 72, 128), f32),
        in_specs=[pl.BlockSpec(memory_space=pltpu.VMEM)] * 5,
        out_specs=pl.BlockSpec(memory_space=pltpu.VMEM),
        scratch_shapes=[
            pltpu.VMEM((line.shape[0] // 2, 256, 256), bf16),
            pltpu.VMEM((2, tile, 256), f32),
            pltpu.VMEM((2, 8, 256), f32),
            pltpu.VMEM((72, 256), f32),
        ],
        compiler_params=pltpu.CompilerParams(vmem_limit_bytes=24 * 2**20),
    )(line, *own, *other)


def combine_kernel(slot_ref, *refs):
    out_ref = refs[-1]
    parts = refs[:-1]
    row = lax.broadcasted_iota(jnp.int32, (72, 128), 0)
    for k in range(out_ref.shape[0]):
        blocks = [p[k] for p in parts]
        tops = [b[DIM + 1 : DIM + 2] for b in blocks]
        top = functools.reduce(jnp.maximum, tops)
        total = sum(b * jnp.exp2(t - top) for b, t in zip(blocks, tops))
        out_ref[slot_ref[k]] = jnp.where(row == DIM + 1, top, total)


def combine(slots, parts):
    vmem = pl.BlockSpec(memory_space=pltpu.VMEM)
    return pl.pallas_call(
        combine_kernel,
        out_shape=jax.ShapeDtypeStruct(parts[0].shape, f32),
        in_specs=[pl.BlockSpec(memory_space=pltpu.SMEM)] + [vmem] * len(parts),
        out_specs=vmem,
        compiler_params=pltpu.CompilerParams(vmem_limit_bytes=8 * 2**20),
        name="combine",
    )(slots, *parts)


def moments_kernel(got_ref, x_ref, label_ref, projected_ref, sums_ref):
    peers, _, cells = got_ref.shape
    top = got_ref[0, DIM : DIM + 8, :][1:2]
    for p in range(1, peers):
        top = jnp.maximum(top, got_ref[p, DIM : DIM + 8, :][1:2])
    total = jnp.zeros((72, cells), f32)
    for p in range(peers):
        block = got_ref[p]
        total = total + block * jnp.exp2(block[DIM + 1 : DIM + 2] - top)
    projected = total[:DIM] / total[DIM : DIM + 1]
    projected_ref[...] = projected
    moved = projected - x_ref[...].astype(f32)
    classes = lax.broadcasted_iota(jnp.int32, (FATES, cells), 0)
    indicator = jnp.where(classes == label_ref[...], 1.0, 0.0)
    across = (((1,), (1,)), ((), ()))
    by_class = lax.dot_general(
        moved, indicator, across, precision=lax.Precision.HIGHEST, preferred_element_type=f32
    )
    padded = jnp.concatenate([moved, jnp.zeros((128 - DIM, cells), f32)], 0)
    second = lax.dot_general(
        moved, padded, across, precision=lax.Precision.HIGHEST, preferred_element_type=f32
    )
    count = jnp.sum(indicator, 1, keepdims=True)
    lane = lax.broadcasted_iota(jnp.int32, (DIM, 128), 1)
    for q in range(FATES // DIM):
        second = jnp.where(lane == DIM + q, count[DIM * q : DIM * (q + 1)], second)
    sums_ref[:8] = by_class[:, :128].reshape(8, 8, 128)
    sums_ref[8:16] = by_class[:, 128:].reshape(8, 8, 128)
    sums_ref[16:24] = second.reshape(8, 8, 128)
    sums_ref[24:] = jnp.zeros((8, 8, 128), f32)


def moments(got, early, labels):
    return pl.pallas_call(
        moments_kernel,
        out_shape=(
            jax.ShapeDtypeStruct(early.shape, f32),
            jax.ShapeDtypeStruct((32, 8, 128), f32),
        ),
        in_specs=[pl.BlockSpec(memory_space=pltpu.VMEM)] * 3,
        out_specs=(pl.BlockSpec(memory_space=pltpu.VMEM),) * 2,
        compiler_params=pltpu.CompilerParams(vmem_limit_bytes=16 * 2**20),
        name="moments",
    )(got, early, labels)


def correlate_kernel(sums_ref, split_ref, out_ref, right, stage, sems, *, cells, block):
    genes = split_ref.shape[0]
    halves = [sums_ref[8 * h : 8 * h + 8].reshape(DIM, 128) for h in range(3)]
    by_class = jnp.concatenate(halves[:2], 1) / cells
    second = halves[2]
    flipped = second.T
    share = jnp.concatenate([flipped[DIM + q : DIM + q + 1] for q in range(FATES // DIM)], 1) / cells
    mean = jnp.sum(by_class, 1, keepdims=True)
    mean_row = jnp.broadcast_to(mean, (DIM, 128)).T[:1, :DIM]
    square = second[:, :DIM] / cells - mean * mean_row
    cross = (by_class - mean * share) / jnp.sqrt(share * (1.0 - share))
    both = jnp.concatenate([cross, square, square], 1)
    high = both.astype(bf16)
    low = (both - high.astype(f32)).astype(bf16)
    right[...] = jnp.concatenate([high, high, low, low], 0)

    def copy(k):
        rows = pl.ds(k * block, block)
        return pltpu.make_async_copy(stage.at[rows], out_ref.at[rows], sems.at[k])

    for k in range(genes // block):
        rows = split_ref[k * block : (k + 1) * block]
        product = jnp.dot(rows, right[...], preferred_element_type=f32)
        halves = rows[:, :128].astype(f32)
        variance = jnp.sum(product[:, FATES:] * halves, 1, keepdims=True) + EPSILON
        stage[k * block : (k + 1) * block] = product[:, :FATES] * (1.0 / jnp.sqrt(variance))
        copy(k).start()
    for k in range(genes // block):
        copy(k).wait()


def correlate(sums, split, cells, block=400):
    genes = split.shape[0]
    return pl.pallas_call(
        functools.partial(correlate_kernel, cells=cells, block=block),
        out_shape=jax.ShapeDtypeStruct((genes, FATES), f32),
        in_specs=[pl.BlockSpec(memory_space=pltpu.VMEM)] * 2,
        out_specs=pl.BlockSpec(memory_space=pl.ANY),
        scratch_shapes=[
            pltpu.VMEM((256, FATES + 128), bf16),
            pltpu.VMEM((genes, FATES), f32),
            pltpu.SemaphoreType.DMA((genes // block,)),
        ],
        compiler_params=pltpu.CompilerParams(vmem_limit_bytes=16 * 2**20),
        name="correlate",
    )(sums, split)


def shift(n, k):
    return [(i, (i + k) % n) for i in range(n)]


def shift_y(k):
    place = [y % 2 * 2 + y // 2 for y in range(4)]
    return [(place[y], place[(y + k) % 4]) for y in range(4)]


def exchange(blocks, axes):
    return lax.all_to_all(blocks, axes, 0, 0, tiled=False)


def spread(block, axes, size):
    return exchange(jnp.broadcast_to(block[None], (size,) + block.shape), axes)


def program(early, late, late_logs, labels, loadings):
    cells = float(early.shape[1] * math.prod(SIZES))
    turned = loadings.T
    high = lax.reduce_precision(turned, 8, 7)
    low = turned - high
    split = jnp.concatenate([high, low, high, low], 1).astype(bf16)

    swap = [(0, 1), (1, 0)]
    late_copies = pack(late, late_logs, SIZES[1])
    late_own = exchange(late_copies, "z")
    late_other = lax.ppermute(late_own, "core", swap)
    line = [early] + [lax.ppermute(early, "x", shift(4, k)) for k in range(1, 4)]
    line = jnp.stack(line)
    turns = [lax.ppermute(line, ("yl", "yh"), shift_y(k)) for k in range(1, 4)]
    back = jnp.arange(4, dtype=jnp.int32)
    slots = ((lax.axis_index("x") - back) % 4).astype(jnp.int32)
    own = ready(late_own)
    other = ready(late_other)
    lines = [line] + turns
    parts = {}
    for k in LINE_ORDER:
        parts[k] = attend_line(lines[k], own, other)
        if k:
            parts[k] = lax.ppermute(parts[k], ("yl", "yh"), shift_y(4 - k))
    got = exchange(combine(slots, [parts[k] for k in range(4)]), "x")
    projected, sums = moments(got, early, labels[None])
    sums = jnp.sum(exchange(sums.reshape(16, 16, 128), PLANE), 0)
    sums = sums + lax.ppermute(sums, "core", swap)
    sums = jnp.sum(spread(sums, "z", SIZES[1]), 0)
    sums = spread(sums, PLANE, 16).reshape(32, 8, 128)
    return projected, correlate(sums, split, cells)


def solution(mesh):
    named = Mesh(mesh.devices.reshape(SIZES), AXES)
    in_specs = (P(None, AXES), P(None, AXES), P(AXES), P(AXES), P())
    out_specs = (P(None, AXES), P())
    return jax.shard_map(
        program, mesh=named, in_specs=in_specs, out_specs=out_specs, check_vma=False
    )
```
